512 devices in a mesh: depth: 16 (over x, y), trans: 32 (over z, core).
Axes of the slice: x: 4, y: 4, z: 16, core: 2. Of those that a mesh axis runs over, the one named last changes fastest.
Arguments:
- flight_fields: bfloat16 [16, 2, 2, 1024, 1024], P('depth', None, None, 'trans'), may hold values from -6 to 6
- top_fields: bfloat16 [2, 2, 1024, 1024], P(None, None, 'trans'), may hold values from -6 to 6
- slowness: float32 [16, 1024, 1024], P('depth', 'trans'), may hold values from 0.5 to 1.5
- ref_slowness: float32 [16], P('depth'), may hold values from 0.6 to 1
- flight_blocks: int32 [16], replicated, may hold values from 128 to 191
- top_block: int32 [1], replicated, may hold values from 0 to 255
Outputs:
- image: float32 [16, 1024, 1024], P('depth', 'trans')
- next_fields: bfloat16 [16, 2, 2, 1024, 1024], P('depth', None, None, 'trans')
The draws below stay inside these ranges and needn't reach their ends.
All inputs are finite; a program needn't handle non-finite values.
Results may differ from the reference program's by a relative error of at most 0.02.
Values may be sent and summed in bfloat16 or wider, within the bound.
A program may use at most 64 MiB of HBM per device.

```python
import math
import jax
import jax.numpy as jnp

NX = 1024
NY = 1024
NFREQ = 256
NZ_DEV = 1
SLABS = 16
NZ = 16
N_DEPTH = 16


def block_law(key):
    base = jax.random.fold_in(key, 701)
    lowest = NFREQ // 2
    highest = 3 * NFREQ // 4 - 1
    values = jax.random.randint(jax.random.fold_in(base, 1), (SLABS,), lowest, highest + 1, dtype=jnp.int32)
    order = jax.random.permutation(jax.random.fold_in(base, 2), SLABS)
    values = values.at[order[0]].set(lowest)
    values = values.at[order[1]].set(highest)
    return values


def slowness_law(key):
    base = jax.random.fold_in(key, 702)
    return jax.random.uniform(base, (NZ,), jnp.float32, 0.6, 1.0)


def draw_flight_blocks(key, part):
    return block_law(key)


def draw_ref_slowness(key, part):
    return slowness_law(key)


def draw_flight_fields(key, part):
    blocks = block_law(key)
    levels = slowness_law(key)
    angular = 4.0 * (blocks.astype(jnp.float32) + 1.0) / NFREQ
    first_ref = levels[jnp.arange(SLABS, dtype=jnp.int32) * NZ_DEV]
    radius = angular * first_ref
    waves = 6
    base = jax.random.fold_in(key, 703)
    small_shape = (SLABS, 2, waves)
    theta = jax.random.uniform(jax.random.fold_in(base, 1), small_shape, jnp.float32, 0.0, 2.0 * math.pi)
    offset = jax.random.uniform(jax.random.fold_in(base, 2), small_shape, jnp.float32, -0.04, 0.04)
    start_phase = jax.random.uniform(jax.random.fold_in(base, 3), small_shape, jnp.float32, 0.0, 2.0 * math.pi)
    full_shape = (SLABS, 2, 2, NX, NY)
    amplitude = jnp.full(small_shape, 0.4, jnp.float32)
    noise = 0.5 * jax.random.truncated_normal(jax.random.fold_in(base, 5), -6.0, 6.0, full_shape, jnp.float32)
    wave_len = radius[:, None, None] + offset
    wave_x = wave_len * jnp.cos(theta)
    wave_y = wave_len * jnp.sin(theta)
    x_pos = jnp.arange(NX, dtype=jnp.float32)
    y_pos = jnp.arange(NY, dtype=jnp.float32)
    real_sum = jnp.zeros((SLABS, 2, NX, NY), jnp.float32)
    imag_sum = jnp.zeros((SLABS, 2, NX, NY), jnp.float32)
    for index in range(waves):
        phase = wave_x[:, :, index][:, :, None, None] * x_pos[None, None, :, None] + wave_y[:, :, index][:, :, None, None] * y_pos[None, None, None, :] + start_phase[:, :, index][:, :, None, None]
        weight = amplitude[:, :, index][:, :, None, None]
        real_sum = real_sum + weight * jnp.cos(phase)
        imag_sum = imag_sum + weight * jnp.sin(phase)
    cycle_part = jnp.stack([real_sum, imag_sum], axis=2)
    return (cycle_part + noise).astype(jnp.bfloat16)


def shard_levels(own_key, shape, shards, least, high):
    def one(axis_at, shards_of):
        steps = jax.random.uniform(jax.random.fold_in(jax.random.fold_in(own_key, 6), axis_at), (shards_of,), jnp.float32, least / len(shards), high / len(shards))
        return jnp.repeat(jnp.exp(steps), shape[axis_at] // shards_of).reshape((-1,) + (1,) * (len(shape) - axis_at - 1))

    level = one(*shards[0])
    for cut in shards[1:]:
        level = level * one(*cut)
    return level


def gaussian(stream_key, shape, spread, most, shards=(), kind=jnp.bfloat16):
    entries = spread * jax.random.normal(stream_key, shape, jnp.float32)
    if shards:
        entries = entries * shard_levels(stream_key, shape, shards, -0.22, 0.18)
    return jnp.clip(entries, -most, most).astype(kind)


def setup_inputs(seed: int = 0) -> dict:
    key_of = jax.random.split(jax.random.key(seed), 7)
    return {
        "flight_fields": draw_flight_fields(jax.random.fold_in(key_of[6], 71), 0),
        "top_fields": gaussian(key_of[1], (2, 2, NX, NY), 1.0, 6.0, ((2, 32),)),
        "slowness": jnp.clip(0.5 + 1.0 * jax.random.uniform(key_of[2], (NZ, NX, NY), jnp.float32) ** shard_levels(key_of[2], (NZ, NX, NY), ((0, 16), (1, 32)), -0.2, 0.2), 0.5, 1.5),
        "ref_slowness": draw_ref_slowness(jax.random.fold_in(key_of[6], 71), 0),
        "flight_blocks": draw_flight_blocks(jax.random.fold_in(key_of[6], 71), 0),
        "top_block": jax.random.randint(key_of[5], (1,), 0, NFREQ).astype(jnp.int32),
    }


omega_top = 4.0
step_length = 0.5

def make_table(length):
    positions = jnp.arange(length, dtype=jnp.int32)
    product = positions[:, None] * positions[None, :] % length
    angles = product.astype(jnp.float32) * (2.0 * math.pi / length)
    scaling = 1.0 / math.sqrt(length)
    return (jnp.concatenate([jnp.cos(angles), jnp.sin(angles)], axis=1) * scaling).astype(jnp.bfloat16)

def wavenumber(positions, length):
    signed = jnp.where(positions < length // 2, positions, positions - length)
    return signed.astype(jnp.float32) * (2.0 * math.pi / length)

def mix(product, along, half_size, orient):
    cosine_part = jax.lax.slice_in_dim(product, 0, half_size, axis=along)
    sine_part = jax.lax.slice_in_dim(product, half_size, 2 * half_size, axis=along)
    real_part = cosine_part[:, 0] + orient * sine_part[:, 1]
    imag_part = cosine_part[:, 1] - orient * sine_part[:, 0]
    return jnp.stack([real_part, imag_part], axis=1)

def rotate(values, cosines, sine_vals):
    real_part = values[:, 0] * cosines - values[:, 1] * sine_vals
    imag_part = values[:, 0] * sine_vals + values[:, 1] * cosines
    return jnp.stack([real_part, imag_part], axis=1)

def spectral(angular, reference_s, wave_x, wave_y):
    quad = (angular * reference_s) ** 2 - wave_x * wave_x - wave_y * wave_y
    travel = jnp.sqrt(jnp.maximum(quad, 0.0)) * step_length
    damping = jnp.exp(-jnp.sqrt(jnp.maximum(-quad, 0.0)) * step_length)
    cosines = damping * jnp.cos(travel)
    sine_vals = damping * jnp.sin(travel)
    return (jnp.stack([cosines, cosines]), jnp.stack([sine_vals, -sine_vals]))

def advance_plane(fields, angular, reference_s, slab_slow, table_x, table_y):
    float_x = table_x.astype(jnp.float32)
    float_y = table_y.astype(jnp.float32)
    product = jnp.einsum('fcxy,yk->fcxk', fields.astype(jnp.float32), float_y)
    first = mix(product, 3, NY, 1.0).astype(jnp.bfloat16)
    product = jnp.einsum('fcxk,xm->fcmk', first.astype(jnp.float32), float_x)
    spectrum = mix(product, 2, NX, 1.0)
    wave_x = wavenumber(jnp.arange(NX, dtype=jnp.int32), NX)[:, None]
    wave_y = wavenumber(jnp.arange(NY, dtype=jnp.int32), NY)[None, :]
    cosines, sine_vals = spectral(angular, reference_s, wave_x, wave_y)
    shifted = rotate(spectrum, cosines, sine_vals).astype(jnp.bfloat16)
    product = jnp.einsum('fcmk,mx->fcxk', shifted.astype(jnp.float32), float_x)
    back_x = mix(product, 2, NX, -1.0).astype(jnp.bfloat16)
    product = jnp.einsum('fcxk,ky->fcxy', back_x.astype(jnp.float32), float_y)
    space = mix(product, 3, NY, -1.0)
    rotation = angular * (slab_slow - reference_s) * step_length
    cos_r = jnp.cos(rotation)
    sin_r = jnp.sin(rotation)
    stepped = rotate(space, jnp.stack([cos_r, cos_r]), jnp.stack([sin_r, -sin_r])).astype(jnp.bfloat16)
    values = stepped.astype(jnp.float32)
    level_term = values[0, 0] * values[1, 0] + values[0, 1] * values[1, 1]
    return (stepped, level_term)

def reference(flight_fields, top_fields, slowness, ref_slowness, flight_blocks, top_block):
    table_x = make_table(NX)
    table_y = make_table(NY)

    def advance(fields, block_id, slab):
        angular = omega_top * (block_id.astype(jnp.float32) + 1.0) / NFREQ
        terms = []
        for level_idx in range(NZ_DEV):
            depth_level = slab * NZ_DEV + level_idx
            fields, level_term = advance_plane(fields, angular, ref_slowness[depth_level], slowness[depth_level], table_x, table_y)
            terms.append(level_term)
        return (fields, jnp.stack(terms))
    after_first = []
    first_terms = []
    for slab in range(N_DEPTH):
        stepped, terms = advance(flight_fields[slab], flight_blocks[slab], slab)
        after_first.append(stepped)
        first_terms.append(terms)
    second = []
    images = []
    for slab in range(N_DEPTH):
        if slab == 0:
            incoming = top_fields
            block_id = top_block[0]
        else:
            incoming = after_first[slab - 1]
            block_id = flight_blocks[slab - 1]
        stepped, terms = advance(incoming, block_id, slab)
        second.append(stepped)
        images.append(first_terms[slab] + terms)
    return (jnp.concatenate(images, axis=0), jnp.stack(second))
```

```python
import math

import jax
import jax.numpy as jnp
import ml_dtypes
import numpy as np
from jax import lax
from jax.experimental import pallas as pl
from jax.experimental.pallas import tpu as pltpu
from jax.sharding import PartitionSpec as P

MESH = pl.DeviceIdType.MESH
N = 1024
NFREQ = 256
DEPTH = 16
TRANS = 32
CHIPS = TRANS // 2
ROWS = N // TRANS
HALF = N // CHIPS
CHUNK = 256
omega_top = 4.0
step_length = 0.5


def make_table(length):
    positions = np.arange(length, dtype=np.int64)
    product = positions[:, None] * positions[None, :] % length
    angles = product.astype(np.float32) * np.float32(2.0 * math.pi / length)
    scaling = np.float32(1.0 / math.sqrt(length))
    table = np.concatenate([np.cos(angles), np.sin(angles)], axis=1) * scaling
    return table.astype(ml_dtypes.bfloat16)


def sine(x):
    y = x * x
    p = jnp.float32(1.0 / 355687428096000.0)
    for factorial in (1307674368000.0, 6227020800.0, 39916800.0, 362880.0, 5040.0, 120.0, 6.0, 1.0):
        p = 1.0 / factorial - y * p
    return x * p


def cosine(x):
    y = x * x
    p = jnp.float32(1.0 / 20922789888000.0)
    for factorial in (87178291200.0, 479001600.0, 3628800.0, 40320.0, 720.0, 24.0, 2.0, 1.0):
        p = 1.0 / factorial - y * p
    return p


def wavenumber(positions):
    signed = jnp.where(positions < N // 2, positions, positions - N)
    return signed.astype(jnp.float32) * (2.0 * math.pi / N)


def kernel(
    table_hbm, flight_hbm, top_hbm, slow_hbm, ref_s, flight_blocks, top_block,
    image, next_fields,
    table, flight, top, slow, first_image,
    d1, d3, e2, e4, handed,
    sa1, sa2, sa3, sa4, step1,
    lhs1, lhs2, rolled, shifted, back, spec_c, spec_s, rot_c, rot_s,
    load_sem, send_sem, recv_sem,
):
    s = lax.axis_index("depth")
    t = lax.axis_index("trans")
    chip, core = t // 2, lax.rem(t, 2)
    low = lax.broadcasted_iota(jnp.int32, (1, 128), 1) < 64
    plus = jnp.where(low, 1.0, -1.0)

    loads = [
        pltpu.make_async_copy(flight_hbm, flight, load_sem.at[0]),
        pltpu.make_async_copy(table_hbm, table, load_sem.at[1]),
        pltpu.make_async_copy(slow_hbm, slow, load_sem.at[2]),
        pltpu.make_async_copy(top_hbm, top, load_sem.at[3]),
    ]
    for load in loads:
        load.start()

    barrier = pltpu.get_barrier_semaphore()

    @pl.loop(1, TRANS)
    def _(i):
        pl.semaphore_signal(barrier, inc=1, device_id=(s, lax.rem(t + i, TRANS)), device_id_type=MESH)

    for shift in (1, DEPTH - 1):
        pl.semaphore_signal(barrier, inc=1, device_id=(lax.rem(s + shift, DEPTH), t), device_id_type=MESH)

    def remote(src, dst, sem_s, sem_r, dd, tt):
        pltpu.make_async_remote_copy(
            src_ref=src, dst_ref=dst, send_sem=send_sem.at[sem_s], recv_sem=recv_sem.at[sem_r],
            device_id=(dd, tt), device_id_type=MESH,
        ).start()

    def other_chip(j):
        m = (j + 1) // 2
        return lax.rem(chip + 8 + (1 - 2 * lax.rem(j, 2)) * m, CHIPS)

    def send_cols(f, src, dst, sem_s, sem_r):
        place = pl.ds(pl.multiple_of(t * ROWS, ROWS), ROWS)

        @pl.loop(0, CHIPS - 1)
        def _(j):
            q = other_chip(j)
            remote(src.at[q], dst.at[place], sem_s, sem_r, s, 2 * q + f)

        @pl.when(core == f)
        def _():
            pltpu.make_async_copy(src.at[chip], dst.at[place], recv_sem.at[sem_r]).start()

        @pl.when(core != f)
        def _():
            remote(src.at[chip], dst.at[place], sem_s, sem_r, s, 2 * chip + f)

    def sent_cols(f, src, sem_s):
        @pl.when(core == f)
        def _():
            part = src.at[pl.ds(0, CHIPS - 1)]
            pltpu.make_async_copy(part, part, send_sem.at[sem_s]).wait()

        @pl.when(core != f)
        def _():
            pltpu.make_async_copy(src, src, send_sem.at[sem_s]).wait()

    def send_rows(src, dst, sem_s, sem_r):
        @pl.loop(0, CHIPS - 1)
        def _(j):
            q = other_chip(j)
            for c in range(2):
                p = 2 * q + c
                rows = pl.ds(pl.multiple_of(p * ROWS, ROWS), ROWS)
                remote(src.at[rows], dst.at[core, chip], sem_s, sem_r + core, s, p)

        own = pl.ds(pl.multiple_of(t * ROWS, ROWS), ROWS)
        pltpu.make_async_copy(src.at[own], dst.at[core, chip], recv_sem.at[sem_r + core]).start()
        p = 2 * chip + 1 - core
        rows = pl.ds(pl.multiple_of(p * ROWS, ROWS), ROWS)
        remote(src.at[rows], dst.at[core, chip], sem_s, sem_r + core, s, p)

    def sent_rows(src, sem_s):
        part = src.at[pl.ds(0, N - ROWS)]
        pltpu.make_async_copy(part, part, send_sem.at[sem_s]).wait()

    def arrived(dst, sem_r):
        pltpu.make_async_copy(dst, dst, recv_sem.at[sem_r]).wait()

    def y_forward(src, dst):
        u = src[...]
        lhs1[...] = u
        lhs2[0:ROWS] = u[ROWS:]
        lhs2[ROWS:] = -u[:ROWS]

        @pl.loop(0, N // CHUNK)
        def _(j):
            start = pl.multiple_of(j * CHUNK, CHUNK)
            a = jnp.dot(lhs1[...], table[:, pl.ds(start, CHUNK)], preferred_element_type=jnp.float32)
            a += jnp.dot(lhs2[...], table[:, pl.ds(N + start, CHUNK)], preferred_element_type=jnp.float32)
            for h in range(CHUNK // 128):
                re = a[:ROWS, 128 * h : 128 * (h + 1)]
                im = a[ROWS:, 128 * h : 128 * (h + 1)]
                q = j * (CHUNK // 64) + 2 * h
                dst[q] = jnp.where(low, re, pltpu.roll(im, 64, 1)).astype(jnp.bfloat16)
                dst[q + 1] = jnp.where(low, pltpu.roll(re, 64, 1), im).astype(jnp.bfloat16)

    def x_stage(src, dst):
        @pl.loop(0, N // CHUNK)
        def _(i):
            rows = pl.ds(pl.multiple_of(i * CHUNK, CHUNK), CHUNK)
            d = src[rows].astype(jnp.float32)
            rolled[rows] = (pltpu.roll(d, 64, 1) * plus).astype(jnp.bfloat16)

        @pl.loop(0, N // CHUNK)
        def _(i):
            rows = pl.ds(pl.multiple_of(i * CHUNK, CHUNK), CHUNK)
            b = jnp.dot(table[rows, 0:N], src[...], preferred_element_type=jnp.float32)
            b += jnp.dot(table[rows, N : 2 * N], rolled[...], preferred_element_type=jnp.float32)
            b = b * spec_c[rows] + pltpu.roll(b, 64, 1) * spec_s[rows]
            shifted[rows] = b.astype(jnp.bfloat16)
            back[rows] = (pltpu.roll(b, 64, 1) * -plus).astype(jnp.bfloat16)

        @pl.loop(0, N // CHUNK)
        def _(i):
            rows = pl.ds(pl.multiple_of(i * CHUNK, CHUNK), CHUNK)
            c = jnp.dot(table[rows, 0:N], shifted[...], preferred_element_type=jnp.float32)
            c += jnp.dot(table[rows, N : 2 * N], back[...], preferred_element_type=jnp.float32)
            dst[rows] = c.astype(jnp.bfloat16)

    def y_inverse(src, f, finish):
        for j in range(CHIPS // 2):
            even = src[2 * j].astype(jnp.float32)
            odd = src[2 * j + 1].astype(jnp.float32)
            re = jnp.where(low, even, pltpu.roll(odd, 64, 1))
            im = jnp.where(low, pltpu.roll(even, 64, 1), odd)
            lanes = slice(128 * j, 128 * (j + 1))
            lhs1[0:ROWS, lanes] = re.astype(jnp.bfloat16)
            lhs1[ROWS:, lanes] = im.astype(jnp.bfloat16)
            lhs2[0:ROWS, lanes] = (-im).astype(jnp.bfloat16)
            lhs2[ROWS:, lanes] = re.astype(jnp.bfloat16)

        @pl.loop(0, N // CHUNK)
        def _(j):
            start = pl.multiple_of(j * CHUNK, CHUNK)
            v = jnp.dot(lhs1[...], table[:, pl.ds(start, CHUNK)], preferred_element_type=jnp.float32)
            v += jnp.dot(lhs2[...], table[:, pl.ds(N + start, CHUNK)], preferred_element_type=jnp.float32)
            finish(v, pl.ds(start, CHUNK))

    def stepped(v, cols, f):
        sign = 1.0 - 2.0 * f
        re, im = v[:ROWS], v[ROWS:]
        cosines, sines = rot_c[:, cols], rot_s[:, cols] * sign
        return (re * cosines - im * sines).astype(jnp.bfloat16), (re * sines + im * cosines).astype(jnp.bfloat16)

    def angles(block):
        angular = omega_top * (block.astype(jnp.float32) + 1.0) / NFREQ
        reference_s = ref_s[0]
        sign = jnp.where(core == 0, 1.0, -1.0)
        top_q = (angular * reference_s) * (angular * reference_s)
        lanes = lax.broadcasted_iota(jnp.int32, (1, 128), 1)
        wave_y = wavenumber(chip * HALF + lax.rem(lanes, 64))
        signs = -plus * sign

        @pl.loop(0, N // 64)
        def _(i):
            start = pl.multiple_of(i * 64, 64)
            wave_x = wavenumber(start + lax.broadcasted_iota(jnp.int32, (64, 1), 0))
            quad = top_q - wave_x * wave_x - wave_y * wave_y
            size = jnp.sqrt(jnp.abs(quad)) * step_length
            damping = jnp.where(quad < 0.0, jnp.exp(-size), 1.0)
            travel = jnp.where(quad < 0.0, 0.0, size)
            spec_c[pl.ds(start, 64)] = damping * cosine(travel)
            spec_s[pl.ds(start, 64)] = damping * sine(travel) * signs

        @pl.loop(0, N // CHUNK)
        def _(j):
            cols = pl.ds(pl.multiple_of(j * CHUNK, CHUNK), CHUNK)
            rotation = angular * (slow[:, cols] - reference_s) * step_length
            rot_c[:, cols] = cosine(rotation)
            rot_s[:, cols] = sine(rotation)

    loads[0].wait()
    loads[1].wait()
    y_forward(flight.at[0], sa1.at[0])
    pl.semaphore_wait(barrier, TRANS + 1)
    send_cols(0, sa1.at[0], d1, 0, 0)
    y_forward(flight.at[1], sa1.at[1])
    send_cols(1, sa1.at[1], d1, 1, 0)
    loads[2].wait()
    angles(flight_blocks[s])
    arrived(d1, 0)
    x_stage(d1, sa2)
    send_rows(sa2, e2, 2, 1)
    for f in range(2):
        arrived(e2.at[f], 1 + f)

        def finish_first(v, cols):
            re, im = stepped(v, cols, f)
            step1[f, :ROWS, cols] = re
            step1[f, ROWS:, cols] = im
            if f == 1:
                re, im = re.astype(jnp.float32), im.astype(jnp.float32)
                before = step1[0, :, cols].astype(jnp.float32)
                first_image[:, cols] = before[:ROWS] * re + before[ROWS:] * im

        y_inverse(e2.at[f], f, finish_first)

        @pl.when(s < DEPTH - 1)
        def _():
            remote(step1.at[f], handed.at[f], 3 + f, 3 + f, lax.rem(s + 1, DEPTH), t)

        if f == 0:
            loads[3].wait()

        @pl.when(s > 0)
        def _():
            arrived(handed.at[f], 3 + f)

        @pl.when(s == 0)
        def _():
            handed[f] = top[f]

        y_forward(handed.at[f], sa3.at[f])
        send_cols(f, sa3.at[f], d3, 5 + f, 5)

    above = flight_blocks[jnp.maximum(s - 1, 0)]
    angles(jnp.where(s == 0, top_block[0], above))
    arrived(d3, 5)
    x_stage(d3, sa4)
    send_rows(sa4, e4, 7, 6)
    for f in range(2):
        arrived(e4.at[f], 6 + f)

        def finish_second(v, cols):
            re, im = stepped(v, cols, f)
            next_fields[f, :ROWS, cols] = re
            next_fields[f, ROWS:, cols] = im
            if f == 1:
                re, im = re.astype(jnp.float32), im.astype(jnp.float32)
                before = next_fields[0, :, cols].astype(jnp.float32)
                image[:, cols] = first_image[:, cols] + (before[:ROWS] * re + before[ROWS:] * im)

        y_inverse(e4.at[f], f, finish_second)

    for f in range(2):
        sent_cols(f, sa1.at[f], f)
        sent_cols(f, sa3.at[f], 5 + f)

        @pl.when(s < DEPTH - 1)
        def _():
            pltpu.make_async_copy(step1.at[f], step1.at[f], send_sem.at[3 + f]).wait()

    sent_rows(sa2, 2)
    sent_rows(sa4, 7)


def per_device(flight_fields, top_fields, slowness, ref_slowness, flight_blocks, top_block):
    bf16, f32 = jnp.bfloat16, jnp.float32
    hbm = pl.BlockSpec(memory_space=pl.ANY)
    smem = pl.BlockSpec(memory_space=pltpu.SMEM)
    vmem = pl.BlockSpec(memory_space=pltpu.VMEM)
    pairs = (2, 2 * ROWS, N)
    planes = (CHIPS, ROWS, 128)
    image, after_second = pl.pallas_call(
        kernel,
        out_shape=(jax.ShapeDtypeStruct((ROWS, N), f32), jax.ShapeDtypeStruct(pairs, bf16)),
        in_specs=[hbm, hbm, hbm, hbm, smem, smem, smem],
        out_specs=(vmem, vmem),
        scratch_shapes=[
            pltpu.VMEM((N, 2 * N), bf16),
            pltpu.VMEM(pairs, bf16),
            pltpu.VMEM(pairs, bf16),
            pltpu.VMEM((ROWS, N), f32),
            pltpu.VMEM((ROWS, N), f32),
            pltpu.VMEM((N, 128), bf16),
            pltpu.VMEM((N, 128), bf16),
            pltpu.VMEM((2,) + planes, bf16),
            pltpu.VMEM((2,) + planes, bf16),
            pltpu.VMEM(pairs, bf16),
            pltpu.VMEM((2,) + planes, bf16),
            pltpu.VMEM((N, 128), bf16),
            pltpu.VMEM((2,) + planes, bf16),
            pltpu.VMEM((N, 128), bf16),
            pltpu.VMEM(pairs, bf16),
            pltpu.VMEM((2 * ROWS, N), bf16),
            pltpu.VMEM((2 * ROWS, N), bf16),
            pltpu.VMEM((N, 128), bf16),
            pltpu.VMEM((N, 128), bf16),
            pltpu.VMEM((N, 128), bf16),
            pltpu.VMEM((N, 128), f32),
            pltpu.VMEM((N, 128), f32),
            pltpu.VMEM((ROWS, N), f32),
            pltpu.VMEM((ROWS, N), f32),
            pltpu.SemaphoreType.DMA((4,)),
            pltpu.SemaphoreType.DMA((8,)),
            pltpu.SemaphoreType.DMA((8,)),
        ],
        compiler_params=pltpu.CompilerParams(collective_id=0, has_side_effects=True, vmem_limit_bytes=40 << 20),
        name="continuation",
    )(
        jnp.asarray(make_table(N)),
        flight_fields.reshape(pairs),
        top_fields.reshape(pairs),
        slowness.reshape(ROWS, N),
        ref_slowness,
        flight_blocks,
        top_block,
    )
    return image[None], after_second.reshape(1, 2, 2, ROWS, N)


def solution(mesh):
    placed = (
        P("depth", None, None, "trans", None),
        P(None, None, "trans", None),
        P("depth", "trans", None),
        P("depth"),
        P(),
        P(),
    )
    return jax.shard_map(
        per_device,
        mesh=mesh,
        in_specs=placed,
        out_specs=(P("depth", "trans", None), P("depth", None, None, "trans", None)),
        check_vma=False,
    )
```

```python
import math

import jax
import jax.numpy as jnp
import ml_dtypes
import numpy as np
from jax import lax
from jax.experimental import pallas as pl
from jax.experimental.pallas import tpu as pltpu
from jax.sharding import PartitionSpec as P

MESH = pl.DeviceIdType.MESH
N = 1024
NFREQ = 256
DEPTH = 16
TRANS = 32
CHIPS = TRANS // 2
ROWS = N // TRANS
HALF = N // CHIPS
Q = N // 4
BLOCK = 64
omega_top = 4.0
step_length = 0.5
f32 = jnp.float32
bf16 = jnp.bfloat16


def make_tables():
    k = 4 * np.arange(Q)[None, :, None] + np.arange(4)[:, None, None]
    angles = (k * np.arange(Q)[None, None, :] % N) * (2.0 * math.pi / N)
    parts = np.stack([np.cos(angles), np.sin(angles)], axis=1) / math.sqrt(N)
    stacked = parts.reshape(4, 2 * Q, Q)
    flipped = parts.transpose(0, 1, 3, 2).reshape(4, 2 * Q, Q)
    return stacked.astype(ml_dtypes.bfloat16), flipped.astype(ml_dtypes.bfloat16)


def sine(x):
    y = x * x
    p = 1.0 / 355687428096000.0
    for factorial in (1307674368000.0, 6227020800.0, 39916800.0, 362880.0, 5040.0, 120.0, 6.0, 1.0):
        p = 1.0 / factorial - y * p
    return x * p


def cosine(x):
    y = x * x
    p = 1.0 / 20922789888000.0
    for factorial in (87178291200.0, 479001600.0, 3628800.0, 40320.0, 720.0, 24.0, 2.0, 1.0):
        p = 1.0 / factorial - y * p
    return p


def wavenumber(positions):
    signed = jnp.where(positions < N // 2, positions, positions - N)
    return signed.astype(f32) * (2.0 * math.pi / N)


def low_lanes():
    return lax.broadcasted_iota(jnp.int32, (1, 128), 1) < 64


def times_i(v):
    return pltpu.roll(v, 64, 1) * jnp.where(low_lanes(), -1.0, 1.0)


def turned(v):
    return jnp.concatenate([-v[ROWS:], v[:ROWS]], axis=0)


def y_forward(u, tables, dst):
    low = low_lanes()
    u0, u1, u2, u3 = (u[:, Q * j : Q * (j + 1)].astype(f32) for j in range(4))
    a, b, c, d = u0 + u2, u1 + u3, u0 - u2, turned(u1 - u3)
    for r, v in enumerate((a + b, c - d, a - b, c + d)):
        v = v.astype(bf16)
        left = jnp.concatenate([v, -turned(v)], axis=1)
        out = jnp.dot(left, tables[r], preferred_element_type=f32)
        for h in range(2):
            re = out[:ROWS, 128 * h : 128 * (h + 1)]
            im = out[ROWS:, 128 * h : 128 * (h + 1)]
            q = 4 * r + 2 * h
            dst[q] = jnp.where(low, re, pltpu.roll(im, 64, 1)).astype(bf16)
            dst[q + 1] = jnp.where(low, pltpu.roll(re, 64, 1), im).astype(bf16)


def y_inverse(src, tables):
    low = low_lanes()
    w = []
    for r in range(4):
        re, im = [], []
        for h in range(2):
            even = src[4 * r + 2 * h].astype(f32)
            odd = src[4 * r + 2 * h + 1].astype(f32)
            re.append(jnp.where(low, even, pltpu.roll(odd, 64, 1)))
            im.append(jnp.where(low, pltpu.roll(even, 64, 1), odd))
        v = jnp.concatenate([jnp.concatenate(re, axis=1), jnp.concatenate(im, axis=1)], axis=0).astype(bf16)
        left = jnp.concatenate([v, turned(v)], axis=1)
        w.append(jnp.dot(left, tables[r], preferred_element_type=f32))
    a, b, c, d = w[0] + w[2], w[1] + w[3], w[0] - w[2], turned(w[1] - w[3])
    return a + b, c + d, a - b, c - d


def x_stage(src, dst, tables, flipped, spec_c, spec_s, v_ref, g_ref, w_ref):
    for i in range(Q // BLOCK):
        rows = slice(BLOCK * i, BLOCK * (i + 1))
        u0, u1, u2, u3 = (src[Q * j + BLOCK * i : Q * j + BLOCK * (i + 1)].astype(f32) for j in range(4))
        a, b, c, d = u0 + u2, u1 + u3, u0 - u2, times_i(u1 - u3)
        for r, v in enumerate((a + b, c - d, a - b, c + d)):
            v_ref[r, rows] = v.astype(bf16)
    for r in range(4):
        out = jnp.dot(tables[r], v_ref[r], preferred_element_type=f32)
        p, q = out[:Q], out[Q:]
        cosines, sines = spec_c[Q * r : Q * (r + 1)], spec_s[Q * r : Q * (r + 1)]
        g_ref[r] = (p * cosines + q * sines + times_i(p * sines - q * cosines)).astype(bf16)
    for r in range(4):
        w_ref[r] = jnp.dot(flipped[r], g_ref[r], preferred_element_type=f32)
    for i in range(Q // BLOCK):
        p = [w_ref[r, BLOCK * i : BLOCK * (i + 1)] for r in range(4)]
        q = [w_ref[r, Q + BLOCK * i : Q + BLOCK * (i + 1)] for r in range(4)]
        pa, pb, pc, pd = p[0] + p[2], p[1] + p[3], p[0] - p[2], p[1] - p[3]
        qa, qb, qc, qd = q[0] + q[2], q[1] + q[3], q[0] - q[2], q[1] - q[3]
        pairs = ((pa + pb, qa + qb), (pc - qd, qc + pd), (pa - pb, qa - qb), (pc + qd, qc - pd))
        for j, (re, im) in enumerate(pairs):
            dst[Q * j + BLOCK * i : Q * j + BLOCK * (i + 1)] = (re + times_i(im)).astype(bf16)


def spectral(angular, reference_s, chip, sign, spec_c, spec_s):
    square = (angular * reference_s) * (angular * reference_s)
    lanes = lax.broadcasted_iota(jnp.int32, (1, 128), 1)
    wave_y = wavenumber(4 * (HALF * lax.rem(chip, 4) + lax.rem(lanes, 64)) + chip // 4)

    @pl.loop(0, N // BLOCK)
    def _(i):
        start = pl.multiple_of(i * BLOCK, BLOCK)
        r, first = i // (Q // BLOCK), lax.rem(i, Q // BLOCK) * BLOCK
        wave_x = wavenumber(4 * (first + lax.broadcasted_iota(jnp.int32, (BLOCK, 1), 0)) + r)
        quad = square - wave_x * wave_x - wave_y * wave_y
        size = jnp.sqrt(jnp.abs(quad)) * step_length
        damping = jnp.where(quad < 0.0, jnp.exp(-size), 1.0)
        travel = jnp.where(quad < 0.0, 0.0, size)
        spec_c[pl.ds(start, BLOCK)] = damping * cosine(travel)
        spec_s[pl.ds(start, BLOCK)] = damping * sine(travel) * sign


def rotations(angular, reference_s, slow, rot_c, rot_s):
    @pl.loop(0, 4)
    def _(j):
        cols = pl.ds(pl.multiple_of(j * Q, Q), Q)
        rotation = angular * (slow[:, cols] - reference_s) * step_length
        rot_c[:, cols] = cosine(rotation)
        rot_s[:, cols] = sine(rotation)


def rotated(v, cosines, sines):
    re, im = v[:ROWS], v[ROWS:]
    return jnp.concatenate([re * cosines - im * sines, re * sines + im * cosines], axis=0).astype(bf16)


def correlation(source, receiver):
    source, receiver = source.astype(f32), receiver.astype(f32)
    return source[:ROWS] * receiver[:ROWS] + source[ROWS:] * receiver[ROWS:]


def kernel(
    tables_hbm, flipped_hbm, flight_hbm, top_hbm, slow_hbm, ref_s, flight_blocks, top_block,
    image, next_fields,
    tables, flipped, flight, top, slow, first_image,
    d1, d3, e2, e4, sa1, sa2, sa3, sa4, step1,
    v_ref, g_ref, w_ref, spec_c, spec_s, rot_c, rot_s,
    load_sem, send_sem, recv_sem,
):
    s = lax.axis_index("depth")
    t = lax.axis_index("trans")
    chip, core = t // 2, lax.rem(t, 2)
    below, above = lax.rem(s + 1, DEPTH), lax.rem(s + DEPTH - 1, DEPTH)

    barrier = pltpu.get_barrier_semaphore()

    @pl.loop(1, TRANS)
    def _(i):
        pl.semaphore_signal(barrier, inc=1, device_id=(s, lax.rem(t + i, TRANS)), device_id_type=MESH)

    @pl.loop(0, TRANS)
    def _(i):
        pl.semaphore_signal(barrier, inc=1, device_id=(below, i), device_id_type=MESH)
        pl.semaphore_signal(barrier, inc=1, device_id=(above, i), device_id_type=MESH)

    loads = [
        pltpu.make_async_copy(src, dst, load_sem.at[i])
        for i, (src, dst) in enumerate(
            ((flight_hbm, flight), (flipped_hbm, flipped), (slow_hbm, slow), (tables_hbm, tables), (top_hbm, top))
        )
    ]
    for load in loads:
        load.start()

    def remote(src, dst, sem_s, sem_r, dd, tt):
        pltpu.make_async_remote_copy(
            src_ref=src, dst_ref=dst, send_sem=send_sem.at[sem_s], recv_sem=recv_sem.at[sem_r],
            device_id=(dd, tt), device_id_type=MESH,
        ).start()

    def other_chip(j):
        m = (j + 1) // 2
        return lax.rem(chip + 8 + (1 - 2 * lax.rem(j, 2)) * m, CHIPS)

    place = pl.ds(pl.multiple_of(t * ROWS, ROWS), ROWS)

    def send_cols(f, src, dst, sem_s, sem_r):
        @pl.loop(0, CHIPS - 1)
        def _(j):
            q = other_chip(j)
            remote(src.at[q], dst.at[place], sem_s, sem_r, s, 2 * q + f)

        @pl.when(core == f)
        def _():
            pltpu.make_async_copy(src.at[chip], dst.at[place], recv_sem.at[sem_r]).start()

        @pl.when(core != f)
        def _():
            remote(src.at[chip], dst.at[place], sem_s, sem_r, s, 2 * chip + f)

    def sent_cols(f, src, sem_s):
        @pl.when(core == f)
        def _():
            part = src.at[pl.ds(0, CHIPS - 1)]
            pltpu.make_async_copy(part, part, send_sem.at[sem_s]).wait()

        @pl.when(core != f)
        def _():
            sent(src, sem_s)

    def send_below(f, src, dst, sem_s, sem_r):
        @pl.loop(0, CHIPS)
        def _(j):
            q = other_chip(j)
            remote(src.at[q], dst.at[place], sem_s, sem_r, below, 2 * q + f)

    def send_rows(src, dst, sem_s, sem_r):
        @pl.loop(0, CHIPS - 1)
        def _(j):
            q = other_chip(j)
            for c in range(2):
                p = 2 * q + c
                rows = pl.ds(pl.multiple_of(p * ROWS, ROWS), ROWS)
                remote(src.at[rows], dst.at[core, chip], sem_s, sem_r + core, s, p)

        pltpu.make_async_copy(src.at[place], dst.at[core, chip], recv_sem.at[sem_r + core]).start()
        p = 2 * chip + 1 - core
        rows = pl.ds(pl.multiple_of(p * ROWS, ROWS), ROWS)
        remote(src.at[rows], dst.at[core, chip], sem_s, sem_r + core, s, p)

    def sent(src, sem_s):
        pltpu.make_async_copy(src, src, send_sem.at[sem_s]).wait()

    def arrived(dst, sem_r):
        pltpu.make_async_copy(dst, dst, recv_sem.at[sem_r]).wait()

    loads[0].wait()
    loads[1].wait()
    y_forward(flight[0], flipped, sa1.at[0])
    pl.semaphore_wait(barrier, 3 * TRANS - 1)
    send_cols(0, sa1.at[0], d1, 0, 0)
    y_forward(flight[1], flipped, sa1.at[1])
    send_cols(1, sa1.at[1], d1, 1, 0)
    for load in loads[2:]:
        load.wait()
    reference_s = ref_s[0]
    sign = jnp.where(core == 0, 1.0, -1.0)
    first = flight_blocks[s]
    second = jnp.where(s == 0, top_block[0], flight_blocks[jnp.maximum(s - 1, 0)])
    for step, block in enumerate((first, second)):
        angular = omega_top * (block.astype(f32) + 1.0) / NFREQ
        spectral(angular, reference_s, chip, sign, spec_c.at[step], spec_s.at[step])
        rotations(angular, reference_s, slow, rot_c.at[step], rot_s.at[step])
    arrived(d1, 0)
    x_stage(d1, sa2, tables, flipped, spec_c.at[0], spec_s.at[0], v_ref, g_ref, w_ref)
    send_rows(sa2, e2, 2, 1)
    for f in range(2):
        arrived(e2.at[f], 1 + f)
        for j, v in enumerate(y_inverse(e2.at[f], tables)):
            cols = slice(Q * j, Q * (j + 1))
            now = rotated(v, rot_c[0, :, cols], rot_s[0, :, cols] * (1.0 - 2.0 * f))
            if f == 0:
                step1[0, :, cols] = now
            else:
                first_image[:, cols] = correlation(step1[0, :, cols], now)
            step1[1, :, cols] = jnp.where(s == DEPTH - 1, top[f, :, cols], now)
        y_forward(step1[1], flipped, sa3.at[f])
        send_below(f, sa3.at[f], d3, 3 + f, 3)

    arrived(d3, 3)
    x_stage(d3, sa4, tables, flipped, spec_c.at[1], spec_s.at[1], v_ref, g_ref, w_ref)
    send_rows(sa4, e4, 5, 4)
    for f in range(2):
        arrived(e4.at[f], 4 + f)
        for j, v in enumerate(y_inverse(e4.at[f], tables)):
            cols = slice(Q * j, Q * (j + 1))
            now = rotated(v, rot_c[1, :, cols], rot_s[1, :, cols] * (1.0 - 2.0 * f))
            next_fields[f, :, cols] = now
            if f == 1:
                image[:, cols] = first_image[:, cols] + correlation(next_fields[0, :, cols], now)

    for f in range(2):
        sent_cols(f, sa1.at[f], f)
        sent(sa3.at[f], 3 + f)
    for src, sem in ((sa2, 2), (sa4, 5)):
        sent(src.at[pl.ds(0, N - ROWS)], sem)


def per_device(flight_fields, top_fields, slowness, ref_slowness, flight_blocks, top_block):
    hbm = pl.BlockSpec(memory_space=pltpu.HBM)
    smem = pl.BlockSpec(memory_space=pltpu.SMEM)
    vmem = pl.BlockSpec(memory_space=pltpu.VMEM)
    pairs = (2, 2 * ROWS, N)
    planes = (2, CHIPS, ROWS, 128)
    stacked, flipped = make_tables()
    image, after_second = pl.pallas_call(
        kernel,
        out_shape=(jax.ShapeDtypeStruct((ROWS, N), f32), jax.ShapeDtypeStruct(pairs, bf16)),
        in_specs=[hbm] * 5 + [smem] * 3,
        out_specs=(vmem, vmem),
        scratch_shapes=[
            pltpu.VMEM((4, 2 * Q, Q), bf16),
            pltpu.VMEM((4, 2 * Q, Q), bf16),
            pltpu.VMEM(pairs, bf16),
            pltpu.VMEM(pairs, bf16),
            pltpu.VMEM((ROWS, N), f32),
            pltpu.VMEM((ROWS, N), f32),
            pltpu.VMEM((N, 128), bf16),
            pltpu.VMEM((N, 128), bf16),
            pltpu.VMEM(planes, bf16),
            pltpu.VMEM(planes, bf16),
            pltpu.VMEM(planes, bf16),
            pltpu.VMEM((N, 128), bf16),
            pltpu.VMEM(planes, bf16),
            pltpu.VMEM((N, 128), bf16),
            pltpu.VMEM(pairs, bf16),
            pltpu.VMEM((4, Q, 128), bf16),
            pltpu.VMEM((4, Q, 128), bf16),
            pltpu.VMEM((4, 2 * Q, 128), f32),
            pltpu.VMEM((2, N, 128), f32),
            pltpu.VMEM((2, N, 128), f32),
            pltpu.VMEM((2, ROWS, N), f32),
            pltpu.VMEM((2, ROWS, N), f32),
            pltpu.SemaphoreType.DMA((5,)),
            pltpu.SemaphoreType.DMA((6,)),
            pltpu.SemaphoreType.DMA((6,)),
        ],
        compiler_params=pltpu.CompilerParams(collective_id=0, has_side_effects=True, vmem_limit_bytes=60 << 20),
        name="continuation",
    )(
        jnp.asarray(stacked),
        jnp.asarray(flipped),
        flight_fields.reshape(pairs),
        top_fields.reshape(pairs),
        slowness.reshape(ROWS, N),
        ref_slowness,
        flight_blocks,
        top_block,
    )
    return image[None], after_second.reshape(1, 2, 2, ROWS, N)


def solution(mesh):
    placed = (
        P("depth", None, None, "trans", None),
        P(None, None, "trans", None),
        P("depth", "trans", None),
        P("depth"),
        P(),
        P(),
    )
    return jax.shard_map(
        per_device,
        mesh=mesh,
        in_specs=placed,
        out_specs=(P("depth", "trans", None), P("depth", None, None, "trans", None)),
        check_vma=False,
    )
```

```python
import math

import jax
import jax.numpy as jnp
import ml_dtypes
import numpy as np
from jax import lax
from jax.experimental import pallas as pl
from jax.experimental.pallas import tpu as pltpu
from jax.sharding import PartitionSpec as P

MESH = pl.DeviceIdType.MESH
N = 1024
NFREQ = 256
DEPTH = 16
TRANS = 32
CHIPS = TRANS // 2
ROWS = N // TRANS
HALF = N // CHIPS
Q = N // 4
BLOCK = 64
omega_top = 4.0
step_length = 0.5
f32 = jnp.float32
bf16 = jnp.bfloat16


def make_tables():
    k = 4 * np.arange(Q)[None, :, None] + np.arange(4)[:, None, None]
    angles = (k * np.arange(Q)[None, None, :] % N) * (2.0 * math.pi / N)
    parts = np.stack([np.cos(angles), np.sin(angles)], axis=1) / math.sqrt(N)
    stacked = parts.reshape(4, 2 * Q, Q)
    flipped = parts.transpose(0, 1, 3, 2).reshape(4, 2 * Q, Q)
    return stacked.astype(ml_dtypes.bfloat16), flipped.astype(ml_dtypes.bfloat16)


def sine(x):
    y = x * x
    p = 1.0 / 355687428096000.0
    for factorial in (1307674368000.0, 6227020800.0, 39916800.0, 362880.0, 5040.0, 120.0, 6.0, 1.0):
        p = 1.0 / factorial - y * p
    return x * p


def cosine(x):
    y = x * x
    p = 1.0 / 20922789888000.0
    for factorial in (87178291200.0, 479001600.0, 3628800.0, 40320.0, 720.0, 24.0, 2.0, 1.0):
        p = 1.0 / factorial - y * p
    return p


def wavenumber(positions):
    signed = jnp.where(positions < N // 2, positions, positions - N)
    return signed.astype(f32) * (2.0 * math.pi / N)


def low_lanes():
    return lax.broadcasted_iota(jnp.int32, (1, 128), 1) < 64


def times_i(v):
    return pltpu.roll(v, 64, 1) * jnp.where(low_lanes(), -1.0, 1.0)


def turned(v):
    return jnp.concatenate([-v[ROWS:], v[:ROWS]], axis=0)


def y_forward(u, tables, dst):
    low = low_lanes()
    u0, u1, u2, u3 = (u[:, Q * j : Q * (j + 1)].astype(f32) for j in range(4))
    a, b, c, d = u0 + u2, u1 + u3, u0 - u2, turned(u1 - u3)
    for r, v in enumerate((a + b, c - d, a - b, c + d)):
        v = v.astype(bf16)
        left = jnp.concatenate([v, -turned(v)], axis=1)
        out = jnp.dot(left, tables[r], preferred_element_type=f32)
        for h in range(2):
            re = out[:ROWS, 128 * h : 128 * (h + 1)]
            im = out[ROWS:, 128 * h : 128 * (h + 1)]
            q = 4 * r + 2 * h
            dst[q] = jnp.where(low, re, pltpu.roll(im, 64, 1)).astype(bf16)
            dst[q + 1] = jnp.where(low, pltpu.roll(re, 64, 1), im).astype(bf16)


def y_inverse(src, tables):
    low = low_lanes()
    w = []
    for r in range(4):
        re, im = [], []
        for h in range(2):
            even = src[4 * r + 2 * h].astype(f32)
            odd = src[4 * r + 2 * h + 1].astype(f32)
            re.append(jnp.where(low, even, pltpu.roll(odd, 64, 1)))
            im.append(jnp.where(low, pltpu.roll(even, 64, 1), odd))
        v = jnp.concatenate([jnp.concatenate(re, axis=1), jnp.concatenate(im, axis=1)], axis=0).astype(bf16)
        left = jnp.concatenate([v, turned(v)], axis=1)
        w.append(jnp.dot(left, tables[r], preferred_element_type=f32))
    a, b, c, d = w[0] + w[2], w[1] + w[3], w[0] - w[2], turned(w[1] - w[3])
    return a + b, c + d, a - b, c - d


def x_stage(src, dst, tables, flipped, spec_c, spec_s, v_ref, g_ref, w_ref):
    for i in range(Q // BLOCK):
        rows = slice(BLOCK * i, BLOCK * (i + 1))
        u0, u1, u2, u3 = (src[Q * j + BLOCK * i : Q * j + BLOCK * (i + 1)].astype(f32) for j in range(4))
        a, b, c, d = u0 + u2, u1 + u3, u0 - u2, times_i(u1 - u3)
        for r, v in enumerate((a + b, c - d, a - b, c + d)):
            v_ref[r, rows] = v.astype(bf16)
    for r in range(4):
        out = jnp.dot(tables[r], v_ref[r], preferred_element_type=f32)
        p, q = out[:Q], out[Q:]
        cosines, sines = spec_c[Q * r : Q * (r + 1)], spec_s[Q * r : Q * (r + 1)]
        g_ref[r] = (p * cosines + q * sines + times_i(p * sines - q * cosines)).astype(bf16)
    for r in range(4):
        w_ref[r] = jnp.dot(flipped[r], g_ref[r], preferred_element_type=f32)
    for i in range(Q // BLOCK):
        p = [w_ref[r, BLOCK * i : BLOCK * (i + 1)] for r in range(4)]
        q = [w_ref[r, Q + BLOCK * i : Q + BLOCK * (i + 1)] for r in range(4)]
        pa, pb, pc, pd = p[0] + p[2], p[1] + p[3], p[0] - p[2], p[1] - p[3]
        qa, qb, qc, qd = q[0] + q[2], q[1] + q[3], q[0] - q[2], q[1] - q[3]
        pairs = ((pa + pb, qa + qb), (pc - qd, qc + pd), (pa - pb, qa - qb), (pc + qd, qc - pd))
        for j, (re, im) in enumerate(pairs):
            dst[Q * j + BLOCK * i : Q * j + BLOCK * (i + 1)] = (re + times_i(im)).astype(bf16)


def spectral(angular, reference_s, chip, sign, spec_c, spec_s):
    square = (angular * reference_s) * (angular * reference_s)
    lanes = lax.broadcasted_iota(jnp.int32, (1, 128), 1)
    wave_y = wavenumber(4 * (HALF * lax.rem(chip, 4) + lax.rem(lanes, 64)) + chip // 4)

    @pl.loop(0, N // BLOCK)
    def _(i):
        start = pl.multiple_of(i * BLOCK, BLOCK)
        r, first = i // (Q // BLOCK), lax.rem(i, Q // BLOCK) * BLOCK
        wave_x = wavenumber(4 * (first + lax.broadcasted_iota(jnp.int32, (BLOCK, 1), 0)) + r)
        quad = square - wave_x * wave_x - wave_y * wave_y
        size = jnp.sqrt(jnp.abs(quad)) * step_length
        damping = jnp.where(quad < 0.0, jnp.exp(-size), 1.0)
        travel = jnp.where(quad < 0.0, 0.0, size)
        spec_c[pl.ds(start, BLOCK)] = damping * cosine(travel)
        spec_s[pl.ds(start, BLOCK)] = damping * sine(travel) * sign


def rotations(angular, reference_s, slow, rot_c, rot_s):
    @pl.loop(0, 4)
    def _(j):
        cols = pl.ds(pl.multiple_of(j * Q, Q), Q)
        rotation = angular * (slow[:, cols] - reference_s) * step_length
        rot_c[:, cols] = cosine(rotation)
        rot_s[:, cols] = sine(rotation)


def rotated(v, cosines, sines):
    re, im = v[:ROWS], v[ROWS:]
    return jnp.concatenate([re * cosines - im * sines, re * sines + im * cosines], axis=0).astype(bf16)


def correlation(source, receiver):
    source, receiver = source.astype(f32), receiver.astype(f32)
    return source[:ROWS] * receiver[:ROWS] + source[ROWS:] * receiver[ROWS:]


def kernel(
    tables_hbm, flipped_hbm, flight_hbm, top_hbm, slow_hbm, ref_s, flight_blocks, top_block,
    image, next_fields,
    tables, flipped, flight, top, slow, first_image,
    d1, d3, e2, e4, sa1, sa2, sa3, sa4, step1,
    v_ref, g_ref, w_ref, spec_c, spec_s, rot_c, rot_s,
    load_sem, send_sem, recv_sem, entered,
):
    s = lax.axis_index("depth")
    t = lax.axis_index("trans")
    chip, core = t // 2, lax.rem(t, 2)
    below, above = lax.rem(s + 1, DEPTH), lax.rem(s + DEPTH - 1, DEPTH)

    loads = [
        pltpu.make_async_copy(src, dst, load_sem.at[i])
        for i, (src, dst) in enumerate(
            ((flight_hbm, flight), (flipped_hbm, flipped), (slow_hbm, slow), (tables_hbm, tables), (top_hbm, top))
        )
    ]
    for load in loads[:2]:
        load.start()

    barrier = pltpu.get_barrier_semaphore()

    @pl.loop(1, TRANS)
    def _(i):
        pl.semaphore_signal(barrier, inc=1, device_id=(s, lax.rem(t + i, TRANS)), device_id_type=MESH)

    for neighbour in (below, above):
        pl.semaphore_signal(barrier, inc=1, device_id=(neighbour, t), device_id_type=MESH)

    for load in loads[2:]:
        load.start()

    def remote(src, dst, sem_s, sem_r, dd, tt):
        pltpu.make_async_remote_copy(
            src_ref=src, dst_ref=dst, send_sem=send_sem.at[sem_s], recv_sem=recv_sem.at[sem_r],
            device_id=(dd, tt), device_id_type=MESH,
        ).start()

    def other_chip(j):
        m = (j + 1) // 2
        return lax.rem(chip + 8 + (1 - 2 * lax.rem(j, 2)) * m, CHIPS)

    place = pl.ds(pl.multiple_of(t * ROWS, ROWS), ROWS)

    def send_cols(f, src, dst, sem_s, sem_r):
        @pl.loop(0, CHIPS - 1)
        def _(j):
            q = other_chip(j)
            remote(src.at[q], dst.at[place], sem_s, sem_r, s, 2 * q + f)

        @pl.when(core == f)
        def _():
            pltpu.make_async_copy(src.at[chip], dst.at[place], recv_sem.at[sem_r]).start()

        @pl.when(core != f)
        def _():
            remote(src.at[chip], dst.at[place], sem_s, sem_r, s, 2 * chip + f)

    def sent_cols(f, src, sem_s):
        @pl.when(core == f)
        def _():
            part = src.at[pl.ds(0, CHIPS - 1)]
            pltpu.make_async_copy(part, part, send_sem.at[sem_s]).wait()

        @pl.when(core != f)
        def _():
            sent(src, sem_s)

    def send_below(f, src, dst, sem_s, sem_r):
        @pl.loop(0, CHIPS)
        def _(j):
            q = other_chip(j)
            remote(src.at[q], dst.at[place], sem_s, sem_r, below, 2 * q + f)

    def send_rows(src, dst, sem_s, sem_r):
        @pl.loop(0, CHIPS - 1)
        def _(j):
            q = other_chip(j)
            for c in range(2):
                p = 2 * q + c
                rows = pl.ds(pl.multiple_of(p * ROWS, ROWS), ROWS)
                remote(src.at[rows], dst.at[core, chip], sem_s, sem_r + core, s, p)

        pltpu.make_async_copy(src.at[place], dst.at[core, chip], recv_sem.at[sem_r + core]).start()
        p = 2 * chip + 1 - core
        rows = pl.ds(pl.multiple_of(p * ROWS, ROWS), ROWS)
        remote(src.at[rows], dst.at[core, chip], sem_s, sem_r + core, s, p)

    def sent(src, sem_s):
        pltpu.make_async_copy(src, src, send_sem.at[sem_s]).wait()

    def arrived(dst, sem_r):
        pltpu.make_async_copy(dst, dst, recv_sem.at[sem_r]).wait()

    loads[0].wait()
    loads[1].wait()
    y_forward(flight[0], flipped, sa1.at[0])
    pl.semaphore_wait(barrier, TRANS + 1)
    pl.semaphore_signal(entered, inc=1, device_id=(above, t), device_id_type=MESH)
    send_cols(0, sa1.at[0], d1, 0, 0)
    y_forward(flight[1], flipped, sa1.at[1])
    send_cols(1, sa1.at[1], d1, 1, 0)
    for load in loads[2:]:
        load.wait()
    reference_s = ref_s[0]
    sign = jnp.where(core == 0, 1.0, -1.0)
    first = flight_blocks[s]
    second = jnp.where(s == 0, top_block[0], flight_blocks[jnp.maximum(s - 1, 0)])
    for step, block in enumerate((first, second)):
        angular = omega_top * (block.astype(f32) + 1.0) / NFREQ
        spectral(angular, reference_s, chip, sign, spec_c.at[step], spec_s.at[step])
        rotations(angular, reference_s, slow, rot_c.at[step], rot_s.at[step])
    arrived(d1, 0)
    x_stage(d1, sa2, tables, flipped, spec_c.at[0], spec_s.at[0], v_ref, g_ref, w_ref)
    send_rows(sa2, e2, 2, 1)
    for f in range(2):
        arrived(e2.at[f], 1 + f)
        for j, v in enumerate(y_inverse(e2.at[f], tables)):
            cols = slice(Q * j, Q * (j + 1))
            now = rotated(v, rot_c[0, :, cols], rot_s[0, :, cols] * (1.0 - 2.0 * f))
            if f == 0:
                step1[0, :, cols] = now
            else:
                first_image[:, cols] = correlation(step1[0, :, cols], now)
            step1[1, :, cols] = jnp.where(s == DEPTH - 1, top[f, :, cols], now)
        y_forward(step1[1], flipped, sa3.at[f])
        if f == 0:
            pl.semaphore_wait(entered, 1)
        send_below(f, sa3.at[f], d3, 3 + f, 3)

    arrived(d3, 3)
    x_stage(d3, sa4, tables, flipped, spec_c.at[1], spec_s.at[1], v_ref, g_ref, w_ref)
    send_rows(sa4, e4, 5, 4)
    for f in range(2):
        arrived(e4.at[f], 4 + f)
        for j, v in enumerate(y_inverse(e4.at[f], tables)):
            cols = slice(Q * j, Q * (j + 1))
            now = rotated(v, rot_c[1, :, cols], rot_s[1, :, cols] * (1.0 - 2.0 * f))
            next_fields[f, :, cols] = now
            if f == 1:
                image[:, cols] = first_image[:, cols] + correlation(next_fields[0, :, cols], now)

    for f in range(2):
        sent_cols(f, sa1.at[f], f)
        sent(sa3.at[f], 3 + f)
    for src, sem in ((sa2, 2), (sa4, 5)):
        sent(src.at[pl.ds(0, N - ROWS)], sem)


def per_device(flight_fields, top_fields, slowness, ref_slowness, flight_blocks, top_block):
    hbm = pl.BlockSpec(memory_space=pltpu.HBM)
    smem = pl.BlockSpec(memory_space=pltpu.SMEM)
    vmem = pl.BlockSpec(memory_space=pltpu.VMEM)
    pairs = (2, 2 * ROWS, N)
    planes = (2, CHIPS, ROWS, 128)
    stacked, flipped = make_tables()
    image, after_second = pl.pallas_call(
        kernel,
        out_shape=(jax.ShapeDtypeStruct((ROWS, N), f32), jax.ShapeDtypeStruct(pairs, bf16)),
        in_specs=[hbm] * 5 + [smem] * 3,
        out_specs=(vmem, vmem),
        scratch_shapes=[
            pltpu.VMEM((4, 2 * Q, Q), bf16),
            pltpu.VMEM((4, 2 * Q, Q), bf16),
            pltpu.VMEM(pairs, bf16),
            pltpu.VMEM(pairs, bf16),
            pltpu.VMEM((ROWS, N), f32),
            pltpu.VMEM((ROWS, N), f32),
            pltpu.VMEM((N, 128), bf16),
            pltpu.VMEM((N, 128), bf16),
            pltpu.VMEM(planes, bf16),
            pltpu.VMEM(planes, bf16),
            pltpu.VMEM(planes, bf16),
            pltpu.VMEM((N, 128), bf16),
            pltpu.VMEM(planes, bf16),
            pltpu.VMEM((N, 128), bf16),
            pltpu.VMEM(pairs, bf16),
            pltpu.VMEM((4, Q, 128), bf16),
            pltpu.VMEM((4, Q, 128), bf16),
            pltpu.VMEM((4, 2 * Q, 128), f32),
            pltpu.VMEM((2, N, 128), f32),
            pltpu.VMEM((2, N, 128), f32),
            pltpu.VMEM((2, ROWS, N), f32),
            pltpu.VMEM((2, ROWS, N), f32),
            pltpu.SemaphoreType.DMA((5,)),
            pltpu.SemaphoreType.DMA((6,)),
            pltpu.SemaphoreType.DMA((6,)),
            pltpu.SemaphoreType.REGULAR,
        ],
        compiler_params=pltpu.CompilerParams(collective_id=0, has_side_effects=True, vmem_limit_bytes=60 << 20),
        name="continuation",
    )(
        jnp.asarray(stacked),
        jnp.asarray(flipped),
        flight_fields.reshape(pairs),
        top_fields.reshape(pairs),
        slowness.reshape(ROWS, N),
        ref_slowness,
        flight_blocks,
        top_block,
    )
    return image[None], after_second.reshape(1, 2, 2, ROWS, N)


def solution(mesh):
    placed = (
        P("depth", None, None, "trans", None),
        P(None, None, "trans", None),
        P("depth", "trans", None),
        P("depth"),
        P(),
        P(),
    )
    return jax.shard_map(
        per_device,
        mesh=mesh,
        in_specs=placed,
        out_specs=(P("depth", "trans", None), P("depth", None, None, "trans", None)),
        check_vma=False,
    )
```

```python
import math

import jax
import jax.numpy as jnp
import ml_dtypes
import numpy as np
from jax import lax
from jax.experimental import pallas as pl
from jax.experimental.pallas import tpu as pltpu
from jax.sharding import PartitionSpec as P

MESH = pl.DeviceIdType.MESH
N = 1024
NFREQ = 256
DEPTH = 16
TRANS = 32
CHIPS = TRANS // 2
ROWS = N // TRANS
HALF = N // CHIPS
Q = N // 4
BLOCK = 64
omega_top = 4.0
step_length = 0.5
f32 = jnp.float32
bf16 = jnp.bfloat16


def make_tables():
    k = 4 * np.arange(Q)[None, :, None] + np.arange(4)[:, None, None]
    angles = (k * np.arange(Q)[None, None, :] % N) * (2.0 * math.pi / N)
    parts = np.stack([np.cos(angles), np.sin(angles)], axis=1) / math.sqrt(N)
    stacked = parts.reshape(4, 2 * Q, Q)
    flipped = parts.transpose(0, 1, 3, 2).reshape(4, 2 * Q, Q)
    return stacked.astype(ml_dtypes.bfloat16), flipped.astype(ml_dtypes.bfloat16)


def sine(x):
    y = x * x
    p = 1.0 / 355687428096000.0
    for factorial in (1307674368000.0, 6227020800.0, 39916800.0, 362880.0, 5040.0, 120.0, 6.0, 1.0):
        p = 1.0 / factorial - y * p
    return x * p


def cosine(x):
    y = x * x
    p = 1.0 / 20922789888000.0
    for factorial in (87178291200.0, 479001600.0, 3628800.0, 40320.0, 720.0, 24.0, 2.0, 1.0):
        p = 1.0 / factorial - y * p
    return p


def wavenumber(positions):
    signed = jnp.where(positions < N // 2, positions, positions - N)
    return signed.astype(f32) * (2.0 * math.pi / N)


def low_lanes():
    return lax.broadcasted_iota(jnp.int32, (1, 128), 1) < 64


def times_i(v):
    return pltpu.roll(v, 64, 1) * jnp.where(low_lanes(), -1.0, 1.0)


def turned(v):
    return jnp.concatenate([-v[ROWS:], v[:ROWS]], axis=0)


def y_forward(u, tables, dst):
    low = low_lanes()
    u0, u1, u2, u3 = (u[:, Q * j : Q * (j + 1)].astype(f32) for j in range(4))
    a, b, c, d = u0 + u2, u1 + u3, u0 - u2, turned(u1 - u3)
    for r, v in enumerate((a + b, c - d, a - b, c + d)):
        v = v.astype(bf16)
        left = jnp.concatenate([v, -turned(v)], axis=1)
        out = jnp.dot(left, tables[r], preferred_element_type=f32)
        for h in range(2):
            re = out[:ROWS, 128 * h : 128 * (h + 1)]
            im = out[ROWS:, 128 * h : 128 * (h + 1)]
            q = 4 * r + 2 * h
            dst[q] = jnp.where(low, re, pltpu.roll(im, 64, 1)).astype(bf16)
            dst[q + 1] = jnp.where(low, pltpu.roll(re, 64, 1), im).astype(bf16)


def y_inverse(src, tables):
    low = low_lanes()
    w = []
    for r in range(4):
        re, im = [], []
        for h in range(2):
            even = src[4 * r + 2 * h].astype(f32)
            odd = src[4 * r + 2 * h + 1].astype(f32)
            re.append(jnp.where(low, even, pltpu.roll(odd, 64, 1)))
            im.append(jnp.where(low, pltpu.roll(even, 64, 1), odd))
        v = jnp.concatenate([jnp.concatenate(re, axis=1), jnp.concatenate(im, axis=1)], axis=0).astype(bf16)
        left = jnp.concatenate([v, turned(v)], axis=1)
        w.append(jnp.dot(left, tables[r], preferred_element_type=f32))
    a, b, c, d = w[0] + w[2], w[1] + w[3], w[0] - w[2], turned(w[1] - w[3])
    return a + b, c + d, a - b, c - d


def x_stage(src, dst, tables, flipped, spec_c, spec_s, v_ref, g_ref, w_ref):
    for i in range(Q // BLOCK):
        rows = slice(BLOCK * i, BLOCK * (i + 1))
        u0, u1, u2, u3 = (src[Q * j + BLOCK * i : Q * j + BLOCK * (i + 1)].astype(f32) for j in range(4))
        a, b, c, d = u0 + u2, u1 + u3, u0 - u2, times_i(u1 - u3)
        for r, v in enumerate((a + b, c - d, a - b, c + d)):
            v_ref[r, rows] = v.astype(bf16)
    for r in range(4):
        out = jnp.dot(tables[r], v_ref[r], preferred_element_type=f32)
        p, q = out[:Q], out[Q:]
        cosines, sines = spec_c[Q * r : Q * (r + 1)], spec_s[Q * r : Q * (r + 1)]
        g_ref[r] = (p * cosines + q * sines + times_i(p * sines - q * cosines)).astype(bf16)
    for r in range(4):
        w_ref[r] = jnp.dot(flipped[r], g_ref[r], preferred_element_type=f32)
    for i in range(Q // BLOCK):
        p = [w_ref[r, BLOCK * i : BLOCK * (i + 1)] for r in range(4)]
        q = [w_ref[r, Q + BLOCK * i : Q + BLOCK * (i + 1)] for r in range(4)]
        pa, pb, pc, pd = p[0] + p[2], p[1] + p[3], p[0] - p[2], p[1] - p[3]
        qa, qb, qc, qd = q[0] + q[2], q[1] + q[3], q[0] - q[2], q[1] - q[3]
        pairs = ((pa + pb, qa + qb), (pc - qd, qc + pd), (pa - pb, qa - qb), (pc + qd, qc - pd))
        for j, (re, im) in enumerate(pairs):
            dst[Q * j + BLOCK * i : Q * j + BLOCK * (i + 1)] = (re + times_i(im)).astype(bf16)


def spectral(angular, reference_s, chip, sign, spec_c, spec_s):
    square = (angular * reference_s) * (angular * reference_s)
    lanes = lax.broadcasted_iota(jnp.int32, (1, 128), 1)
    wave_y = wavenumber(4 * (HALF * lax.rem(chip, 4) + lax.rem(lanes, 64)) + chip // 4)

    @pl.loop(0, N // BLOCK)
    def _(i):
        start = pl.multiple_of(i * BLOCK, BLOCK)
        r, first = i // (Q // BLOCK), lax.rem(i, Q // BLOCK) * BLOCK
        wave_x = wavenumber(4 * (first + lax.broadcasted_iota(jnp.int32, (BLOCK, 1), 0)) + r)
        quad = square - wave_x * wave_x - wave_y * wave_y
        size = jnp.sqrt(jnp.abs(quad)) * step_length
        damping = jnp.where(quad < 0.0, jnp.exp(-size), 1.0)
        travel = jnp.where(quad < 0.0, 0.0, size)
        spec_c[pl.ds(start, BLOCK)] = damping * cosine(travel)
        spec_s[pl.ds(start, BLOCK)] = damping * sine(travel) * sign


def rotations(angular, reference_s, slow, rot_c, rot_s):
    @pl.loop(0, 4)
    def _(j):
        cols = pl.ds(pl.multiple_of(j * Q, Q), Q)
        rotation = angular * (slow[:, cols] - reference_s) * step_length
        rot_c[:, cols] = cosine(rotation)
        rot_s[:, cols] = sine(rotation)


def rotated(v, cosines, sines):
    re, im = v[:ROWS], v[ROWS:]
    return jnp.concatenate([re * cosines - im * sines, re * sines + im * cosines], axis=0).astype(bf16)


def correlation(source, receiver):
    source, receiver = source.astype(f32), receiver.astype(f32)
    return source[:ROWS] * receiver[:ROWS] + source[ROWS:] * receiver[ROWS:]


def kernel(
    tables_hbm, flipped_hbm, flight_hbm, top_hbm, slow_hbm, scalars_hbm,
    image, next_fields,
    tables, flipped, flight, top, slow, first_image,
    d1, d3, e2, e4, sa1, sa2, sa3, sa4, step1,
    v_ref, g_ref, w_ref, spec_c, spec_s, rot_c, rot_s,
    scalars, load_sem, send_sem, recv_sem, entered,
):
    s = lax.axis_index("depth")
    t = lax.axis_index("trans")
    chip, core = t // 2, lax.rem(t, 2)
    below, above = lax.rem(s + 1, DEPTH), lax.rem(s + DEPTH - 1, DEPTH)

    loads = [
        pltpu.make_async_copy(src, dst, load_sem.at[i])
        for i, (src, dst) in enumerate(
            ((flight_hbm, flight), (flipped_hbm, flipped), (slow_hbm, slow), (tables_hbm, tables), (top_hbm, top), (scalars_hbm, scalars))
        )
    ]
    for load in loads[:2]:
        load.start()

    barrier = pltpu.get_barrier_semaphore()

    @pl.loop(1, TRANS)
    def _(i):
        pl.semaphore_signal(barrier, inc=1, device_id=(s, lax.rem(t + i, TRANS)), device_id_type=MESH)

    for neighbour in (below, above):
        pl.semaphore_signal(barrier, inc=1, device_id=(neighbour, t), device_id_type=MESH)

    for load in loads[2:]:
        load.start()

    def remote(src, dst, sem_s, sem_r, dd, tt):
        pltpu.make_async_remote_copy(
            src_ref=src, dst_ref=dst, send_sem=send_sem.at[sem_s], recv_sem=recv_sem.at[sem_r],
            device_id=(dd, tt), device_id_type=MESH,
        ).start()

    def other_chip(j):
        m = (j + 1) // 2
        return lax.rem(chip + 8 + (1 - 2 * lax.rem(j, 2)) * m, CHIPS)

    place = pl.ds(pl.multiple_of(t * ROWS, ROWS), ROWS)

    def send_cols(f, src, dst, sem_s, sem_r):
        @pl.loop(0, CHIPS - 1)
        def _(j):
            q = other_chip(j)
            remote(src.at[q], dst.at[place], sem_s, sem_r, s, 2 * q + f)

        @pl.when(core == f)
        def _():
            pltpu.make_async_copy(src.at[chip], dst.at[place], recv_sem.at[sem_r]).start()

        @pl.when(core != f)
        def _():
            remote(src.at[chip], dst.at[place], sem_s, sem_r, s, 2 * chip + f)

    def sent_cols(f, src, sem_s):
        @pl.when(core == f)
        def _():
            part = src.at[pl.ds(0, CHIPS - 1)]
            pltpu.make_async_copy(part, part, send_sem.at[sem_s]).wait()

        @pl.when(core != f)
        def _():
            sent(src, sem_s)

    def send_below(f, src, dst, sem_s, sem_r):
        @pl.loop(0, CHIPS)
        def _(j):
            q = other_chip(j)
            remote(src.at[q], dst.at[place], sem_s, sem_r, below, 2 * q + f)

    def send_rows(src, dst, sem_s, sem_r):
        @pl.loop(0, CHIPS - 1)
        def _(j):
            q = other_chip(j)
            for c in range(2):
                p = 2 * q + c
                rows = pl.ds(pl.multiple_of(p * ROWS, ROWS), ROWS)
                remote(src.at[rows], dst.at[core, chip], sem_s, sem_r + core, s, p)

        pltpu.make_async_copy(src.at[place], dst.at[core, chip], recv_sem.at[sem_r + core]).start()
        p = 2 * chip + 1 - core
        rows = pl.ds(pl.multiple_of(p * ROWS, ROWS), ROWS)
        remote(src.at[rows], dst.at[core, chip], sem_s, sem_r + core, s, p)

    def sent(src, sem_s):
        pltpu.make_async_copy(src, src, send_sem.at[sem_s]).wait()

    def arrived(dst, sem_r):
        pltpu.make_async_copy(dst, dst, recv_sem.at[sem_r]).wait()

    loads[0].wait()
    loads[1].wait()
    y_forward(flight[0], flipped, sa1.at[0])
    pl.semaphore_wait(barrier, TRANS + 1)
    pl.semaphore_signal(entered, inc=1, device_id=(above, t), device_id_type=MESH)
    send_cols(0, sa1.at[0], d1, 0, 0)
    y_forward(flight[1], flipped, sa1.at[1])
    send_cols(1, sa1.at[1], d1, 1, 0)
    for load in loads[2:]:
        load.wait()
    pl.semaphore_wait(entered, 1)

    @pl.when(s == DEPTH - 1)
    def _():
        for f in range(2):
            y_forward(top[f], flipped, sa3.at[f])
            send_below(f, sa3.at[f], d3, 3 + f, 3)

    reference_s = scalars[DEPTH + 1]
    sign = jnp.where(core == 0, 1.0, -1.0)
    first = scalars[s]
    second = jnp.where(s == 0, scalars[DEPTH], scalars[jnp.maximum(s - 1, 0)])
    for step, block in enumerate((first, second)):
        angular = omega_top * (block + 1.0) / NFREQ
        spectral(angular, reference_s, chip, sign, spec_c.at[step], spec_s.at[step])
        rotations(angular, reference_s, slow, rot_c.at[step], rot_s.at[step])
    arrived(d1, 0)
    x_stage(d1, sa2, tables, flipped, spec_c.at[0], spec_s.at[0], v_ref, g_ref, w_ref)
    send_rows(sa2, e2, 2, 1)
    for f in range(2):
        arrived(e2.at[f], 1 + f)
        for j, v in enumerate(y_inverse(e2.at[f], tables)):
            cols = slice(Q * j, Q * (j + 1))
            now = rotated(v, rot_c[0, :, cols], rot_s[0, :, cols] * (1.0 - 2.0 * f))
            step1[f, :, cols] = now
            if f == 1:
                first_image[:, cols] = correlation(step1[0, :, cols], now)

        @pl.when(s < DEPTH - 1)
        def _():
            y_forward(step1[f], flipped, sa3.at[f])
            send_below(f, sa3.at[f], d3, 3 + f, 3)


    arrived(d3, 3)
    x_stage(d3, sa4, tables, flipped, spec_c.at[1], spec_s.at[1], v_ref, g_ref, w_ref)
    send_rows(sa4, e4, 5, 4)
    for f in range(2):
        arrived(e4.at[f], 4 + f)
        for j, v in enumerate(y_inverse(e4.at[f], tables)):
            cols = slice(Q * j, Q * (j + 1))
            now = rotated(v, rot_c[1, :, cols], rot_s[1, :, cols] * (1.0 - 2.0 * f))
            next_fields[f, :, cols] = now
            if f == 1:
                image[:, cols] = first_image[:, cols] + correlation(next_fields[0, :, cols], now)

    for f in range(2):
        sent_cols(f, sa1.at[f], f)
        sent(sa3.at[f], 3 + f)
    for src, sem in ((sa2, 2), (sa4, 5)):
        sent(src.at[pl.ds(0, N - ROWS)], sem)


def per_device(flight_fields, top_fields, slowness, ref_slowness, flight_blocks, top_block):
    hbm = pl.BlockSpec(memory_space=pltpu.HBM)
    vmem = pl.BlockSpec(memory_space=pltpu.VMEM)
    pairs = (2, 2 * ROWS, N)
    planes = (2, CHIPS, ROWS, 128)
    stacked, flipped = make_tables()
    image, after_second = pl.pallas_call(
        kernel,
        out_shape=(jax.ShapeDtypeStruct((ROWS, N), f32), jax.ShapeDtypeStruct(pairs, bf16)),
        in_specs=[hbm] * 6,
        out_specs=(vmem, vmem),
        scratch_shapes=[
            pltpu.VMEM((4, 2 * Q, Q), bf16),
            pltpu.VMEM((4, 2 * Q, Q), bf16),
            pltpu.VMEM(pairs, bf16),
            pltpu.VMEM(pairs, bf16),
            pltpu.VMEM((ROWS, N), f32),
            pltpu.VMEM((ROWS, N), f32),
            pltpu.VMEM((N, 128), bf16),
            pltpu.VMEM((N, 128), bf16),
            pltpu.VMEM(planes, bf16),
            pltpu.VMEM(planes, bf16),
            pltpu.VMEM(planes, bf16),
            pltpu.VMEM((N, 128), bf16),
            pltpu.VMEM(planes, bf16),
            pltpu.VMEM((N, 128), bf16),
            pltpu.VMEM(pairs, bf16),
            pltpu.VMEM((4, Q, 128), bf16),
            pltpu.VMEM((4, Q, 128), bf16),
            pltpu.VMEM((4, 2 * Q, 128), f32),
            pltpu.VMEM((2, N, 128), f32),
            pltpu.VMEM((2, N, 128), f32),
            pltpu.VMEM((2, ROWS, N), f32),
            pltpu.VMEM((2, ROWS, N), f32),
            pltpu.SMEM((DEPTH + 2,), f32),
            pltpu.SemaphoreType.DMA((6,)),
            pltpu.SemaphoreType.DMA((6,)),
            pltpu.SemaphoreType.DMA((6,)),
            pltpu.SemaphoreType.REGULAR,
        ],
        compiler_params=pltpu.CompilerParams(collective_id=0, has_side_effects=True, vmem_limit_bytes=48 << 20),
        name="continuation",
    )(
        *(
            pltpu.with_memory_space_constraint(value, pltpu.HBM)
            for value in (
                jnp.asarray(stacked),
                jnp.asarray(flipped),
                flight_fields.reshape(pairs),
                top_fields.reshape(pairs),
                slowness.reshape(ROWS, N),
                jnp.concatenate([flight_blocks.astype(f32), top_block.astype(f32), ref_slowness]),
            )
        ),
    )
    return image[None], after_second.reshape(1, 2, 2, ROWS, N)


def solution(mesh):
    placed = (
        P("depth", None, None, "trans", None),
        P(None, None, "trans", None),
        P("depth", "trans", None),
        P("depth"),
        P(),
        P(),
    )
    return jax.shard_map(
        per_device,
        mesh=mesh,
        in_specs=placed,
        out_specs=(P("depth", "trans", None), P("depth", None, None, "trans", None)),
        check_vma=False,
    )
```

```python
import math

import jax
import jax.numpy as jnp
import ml_dtypes
import numpy as np
from jax import lax
from jax.experimental import pallas as pl
from jax.experimental.pallas import tpu as pltpu
from jax.sharding import PartitionSpec as P

MESH = pl.DeviceIdType.MESH
N = 1024
NFREQ = 256
DEPTH = 16
TRANS = 32
CHIPS = TRANS // 2
ROWS = N // TRANS
HALF = N // CHIPS
Q = N // 4
BLOCK = 64
omega_top = 4.0
step_length = 0.5
f32 = jnp.float32
bf16 = jnp.bfloat16


def make_tables():
    k = 4 * np.arange(Q)[None, :, None] + np.arange(4)[:, None, None]
    angles = (k * np.arange(Q)[None, None, :] % N) * (2.0 * math.pi / N)
    parts = np.stack([np.cos(angles), np.sin(angles)], axis=1) / math.sqrt(N)
    stacked = parts.reshape(4, 2 * Q, Q)
    flipped = parts.transpose(0, 1, 3, 2).reshape(4, 2 * Q, Q)
    return stacked.astype(ml_dtypes.bfloat16), flipped.astype(ml_dtypes.bfloat16)


def sine(x):
    y = x * x
    p = 1.0 / 355687428096000.0
    for factorial in (1307674368000.0, 6227020800.0, 39916800.0, 362880.0, 5040.0, 120.0, 6.0, 1.0):
        p = 1.0 / factorial - y * p
    return x * p


def cosine(x):
    y = x * x
    p = 1.0 / 20922789888000.0
    for factorial in (87178291200.0, 479001600.0, 3628800.0, 40320.0, 720.0, 24.0, 2.0, 1.0):
        p = 1.0 / factorial - y * p
    return p


def wavenumber(positions):
    signed = jnp.where(positions < N // 2, positions, positions - N)
    return signed.astype(f32) * (2.0 * math.pi / N)


def low_lanes():
    return lax.broadcasted_iota(jnp.int32, (1, 128), 1) < 64


def times_i(v):
    return pltpu.roll(v, 64, 1) * jnp.where(low_lanes(), -1.0, 1.0)


def turned(v):
    return jnp.concatenate([-v[ROWS:], v[:ROWS]], axis=0)


def y_forward(u, tables, dst):
    low = low_lanes()
    u0, u1, u2, u3 = (u[:, Q * j : Q * (j + 1)].astype(f32) for j in range(4))
    a, b, c, d = u0 + u2, u1 + u3, u0 - u2, turned(u1 - u3)
    for r, v in enumerate((a + b, c - d, a - b, c + d)):
        v = v.astype(bf16)
        left = jnp.concatenate([v, -turned(v)], axis=1)
        out = jnp.dot(left, tables[r], preferred_element_type=f32)
        for h in range(2):
            re = out[:ROWS, 128 * h : 128 * (h + 1)]
            im = out[ROWS:, 128 * h : 128 * (h + 1)]
            q = 4 * r + 2 * h
            dst[q] = jnp.where(low, re, pltpu.roll(im, 64, 1)).astype(bf16)
            dst[q + 1] = jnp.where(low, pltpu.roll(re, 64, 1), im).astype(bf16)


def y_inverse(src, tables):
    low = low_lanes()
    w = []
    for r in range(4):
        re, im = [], []
        for h in range(2):
            even = src[4 * r + 2 * h].astype(f32)
            odd = src[4 * r + 2 * h + 1].astype(f32)
            re.append(jnp.where(low, even, pltpu.roll(odd, 64, 1)))
            im.append(jnp.where(low, pltpu.roll(even, 64, 1), odd))
        v = jnp.concatenate([jnp.concatenate(re, axis=1), jnp.concatenate(im, axis=1)], axis=0).astype(bf16)
        left = jnp.concatenate([v, turned(v)], axis=1)
        w.append(jnp.dot(left, tables[r], preferred_element_type=f32))
    a, b, c, d = w[0] + w[2], w[1] + w[3], w[0] - w[2], turned(w[1] - w[3])
    return a + b, c + d, a - b, c - d


def x_stage(src, dst, tables, flipped, spec_c, spec_s, v_ref, g_ref, w_ref):
    for i in range(Q // BLOCK):
        rows = slice(BLOCK * i, BLOCK * (i + 1))
        u0, u1, u2, u3 = (src[Q * j + BLOCK * i : Q * j + BLOCK * (i + 1)].astype(f32) for j in range(4))
        a, b, c, d = u0 + u2, u1 + u3, u0 - u2, times_i(u1 - u3)
        for r, v in enumerate((a + b, c - d, a - b, c + d)):
            v_ref[r, rows] = v.astype(bf16)
    for r in range(4):
        out = jnp.dot(tables[r], v_ref[r], preferred_element_type=f32)
        p, q = out[:Q], out[Q:]
        cosines, sines = spec_c[Q * r : Q * (r + 1)], spec_s[Q * r : Q * (r + 1)]
        g_ref[r] = (p * cosines + q * sines + times_i(p * sines - q * cosines)).astype(bf16)
    for r in range(4):
        w_ref[r] = jnp.dot(flipped[r], g_ref[r], preferred_element_type=f32)
    for i in range(Q // BLOCK):
        p = [w_ref[r, BLOCK * i : BLOCK * (i + 1)] for r in range(4)]
        q = [w_ref[r, Q + BLOCK * i : Q + BLOCK * (i + 1)] for r in range(4)]
        pa, pb, pc, pd = p[0] + p[2], p[1] + p[3], p[0] - p[2], p[1] - p[3]
        qa, qb, qc, qd = q[0] + q[2], q[1] + q[3], q[0] - q[2], q[1] - q[3]
        pairs = ((pa + pb, qa + qb), (pc - qd, qc + pd), (pa - pb, qa - qb), (pc + qd, qc - pd))
        for j, (re, im) in enumerate(pairs):
            dst[Q * j + BLOCK * i : Q * j + BLOCK * (i + 1)] = (re + times_i(im)).astype(bf16)


def spectral(angular, reference_s, chip, sign, spec_c, spec_s):
    square = (angular * reference_s) * (angular * reference_s)
    lanes = lax.broadcasted_iota(jnp.int32, (1, 128), 1)
    wave_y = wavenumber(4 * (HALF * lax.rem(chip, 4) + lax.rem(lanes, 64)) + chip // 4)

    @pl.loop(0, N // BLOCK)
    def _(i):
        start = pl.multiple_of(i * BLOCK, BLOCK)
        r, first = i // (Q // BLOCK), lax.rem(i, Q // BLOCK) * BLOCK
        wave_x = wavenumber(4 * (first + lax.broadcasted_iota(jnp.int32, (BLOCK, 1), 0)) + r)
        quad = square - wave_x * wave_x - wave_y * wave_y
        size = jnp.sqrt(jnp.abs(quad)) * step_length
        damping = jnp.where(quad < 0.0, jnp.exp(-size), 1.0)
        travel = jnp.where(quad < 0.0, 0.0, size)
        spec_c[pl.ds(start, BLOCK)] = damping * cosine(travel)
        spec_s[pl.ds(start, BLOCK)] = damping * sine(travel) * sign


def rotations(angular, reference_s, slow, rot_c, rot_s):
    @pl.loop(0, 4)
    def _(j):
        cols = pl.ds(pl.multiple_of(j * Q, Q), Q)
        rotation = angular * (slow[:, cols] - reference_s) * step_length
        rot_c[:, cols] = cosine(rotation)
        rot_s[:, cols] = sine(rotation)


def rotated(v, cosines, sines):
    re, im = v[:ROWS], v[ROWS:]
    return jnp.concatenate([re * cosines - im * sines, re * sines + im * cosines], axis=0).astype(bf16)


def correlation(source, receiver):
    source, receiver = source.astype(f32), receiver.astype(f32)
    return source[:ROWS] * receiver[:ROWS] + source[ROWS:] * receiver[ROWS:]


def kernel(
    tables_hbm, flipped_hbm, flight_hbm, top_hbm, slow_hbm, blocks_hbm, ref_s, top_block,
    image, next_fields,
    tables, flipped, flight, top, slow, first_image,
    d1, d3, e2, e4, sa1, sa2, sa3, sa4, step1,
    v_ref, g_ref, w_ref, spec_c, spec_s, rot_c, rot_s,
    flight_blocks, load_sem, send_sem, recv_sem, entered,
):
    s = lax.axis_index("depth")
    t = lax.axis_index("trans")
    chip, core = t // 2, lax.rem(t, 2)
    below, above = lax.rem(s + 1, DEPTH), lax.rem(s + DEPTH - 1, DEPTH)

    loads = [
        pltpu.make_async_copy(src, dst, load_sem.at[i])
        for i, (src, dst) in enumerate(
            ((flight_hbm, flight), (flipped_hbm, flipped), (slow_hbm, slow), (tables_hbm, tables), (top_hbm, top), (blocks_hbm, flight_blocks))
        )
    ]
    for load in loads[:2]:
        load.start()

    barrier = pltpu.get_barrier_semaphore()

    @pl.loop(1, TRANS)
    def _(i):
        pl.semaphore_signal(barrier, inc=1, device_id=(s, lax.rem(t + i, TRANS)), device_id_type=MESH)

    for neighbour in (below, above):
        pl.semaphore_signal(barrier, inc=1, device_id=(neighbour, t), device_id_type=MESH)

    for load in loads[2:]:
        load.start()

    def remote(src, dst, sem_s, sem_r, dd, tt):
        pltpu.make_async_remote_copy(
            src_ref=src, dst_ref=dst, send_sem=send_sem.at[sem_s], recv_sem=recv_sem.at[sem_r],
            device_id=(dd, tt), device_id_type=MESH,
        ).start()

    def nth_chip(j):
        half, i = j // 8, lax.rem(j, 8)
        odd = lax.rem(half + chip, 2)
        way = 1 - 2 * lax.rem(i, 2)
        offset = 8 + (1 - odd) * way * 2 * ((i + 1) // 2) - odd * way * (1 + 2 * (i // 2))
        return lax.rem(chip + offset, CHIPS)

    place = pl.ds(pl.multiple_of(t * ROWS, ROWS), ROWS)

    def send_cols(f, src, dst, sem_s, sem_r):
        @pl.loop(0, CHIPS)
        def _(j):
            q = nth_chip(j)

            @pl.when(q != chip)
            def _():
                remote(src.at[q], dst.at[place], sem_s, sem_r, s, 2 * q + f)

        @pl.when(core == f)
        def _():
            pltpu.make_async_copy(src.at[chip], dst.at[place], recv_sem.at[sem_r]).start()

        @pl.when(core != f)
        def _():
            remote(src.at[chip], dst.at[place], sem_s, sem_r, s, 2 * chip + f)

    def sent_cols(f, src, sem_s):
        @pl.when(core == f)
        def _():
            part = src.at[pl.ds(0, CHIPS - 1)]
            pltpu.make_async_copy(part, part, send_sem.at[sem_s]).wait()

        @pl.when(core != f)
        def _():
            sent(src, sem_s)

    def send_below(f, src, dst, sem_s, sem_r):
        @pl.loop(0, CHIPS)
        def _(j):
            q = nth_chip(j)
            remote(src.at[q], dst.at[place], sem_s, sem_r, below, 2 * q + f)

    def send_rows(src, dst, sem_s, sem_r):
        @pl.loop(0, CHIPS)
        def _(j):
            q = nth_chip(j)

            @pl.when(q != chip)
            def _():
                for c in range(2):
                    p = 2 * q + c
                    rows = pl.ds(pl.multiple_of(p * ROWS, ROWS), ROWS)
                    remote(src.at[rows], dst.at[core, chip], sem_s, sem_r + core, s, p)

        pltpu.make_async_copy(src.at[place], dst.at[core, chip], recv_sem.at[sem_r + core]).start()
        p = 2 * chip + 1 - core
        rows = pl.ds(pl.multiple_of(p * ROWS, ROWS), ROWS)
        remote(src.at[rows], dst.at[core, chip], sem_s, sem_r + core, s, p)

    def sent(src, sem_s):
        pltpu.make_async_copy(src, src, send_sem.at[sem_s]).wait()

    def arrived(dst, sem_r):
        pltpu.make_async_copy(dst, dst, recv_sem.at[sem_r]).wait()

    loads[0].wait()
    loads[1].wait()
    y_forward(flight[0], flipped, sa1.at[0])
    pl.semaphore_wait(barrier, TRANS + 1)
    pl.semaphore_signal(entered, inc=1, device_id=(above, t), device_id_type=MESH)
    send_cols(0, sa1.at[0], d1, 0, 0)
    y_forward(flight[1], flipped, sa1.at[1])
    send_cols(1, sa1.at[1], d1, 1, 0)
    for load in loads[2:]:
        load.wait()
    pl.semaphore_wait(entered, 1)

    @pl.when(s == DEPTH - 1)
    def _():
        for f in range(2):
            y_forward(top[f], flipped, sa3.at[f])
            send_below(f, sa3.at[f], d3, 3 + f, 3)

    reference_s = ref_s[0]
    sign = jnp.where(core == 0, 1.0, -1.0)
    first = flight_blocks[s]
    second = jnp.where(s == 0, top_block[0], flight_blocks[jnp.maximum(s - 1, 0)])
    for step, block in enumerate((first, second)):
        angular = omega_top * (block.astype(f32) + 1.0) / NFREQ
        spectral(angular, reference_s, chip, sign, spec_c.at[step], spec_s.at[step])
        rotations(angular, reference_s, slow, rot_c.at[step], rot_s.at[step])
    arrived(d1, 0)
    x_stage(d1, sa2, tables, flipped, spec_c.at[0], spec_s.at[0], v_ref, g_ref, w_ref)
    send_rows(sa2, e2, 2, 1)
    for f in range(2):
        arrived(e2.at[f], 1 + f)
        for j, v in enumerate(y_inverse(e2.at[f], tables)):
            cols = slice(Q * j, Q * (j + 1))
            now = rotated(v, rot_c[0, :, cols], rot_s[0, :, cols] * (1.0 - 2.0 * f))
            step1[f, :, cols] = now
            if f == 1:
                first_image[:, cols] = correlation(step1[0, :, cols], now)

        @pl.when(s < DEPTH - 1)
        def _():
            y_forward(step1[f], flipped, sa3.at[f])
            send_below(f, sa3.at[f], d3, 3 + f, 3)


    arrived(d3, 3)
    x_stage(d3, sa4, tables, flipped, spec_c.at[1], spec_s.at[1], v_ref, g_ref, w_ref)
    send_rows(sa4, e4, 5, 4)
    for f in range(2):
        arrived(e4.at[f], 4 + f)
        for j, v in enumerate(y_inverse(e4.at[f], tables)):
            cols = slice(Q * j, Q * (j + 1))
            now = rotated(v, rot_c[1, :, cols], rot_s[1, :, cols] * (1.0 - 2.0 * f))
            next_fields[f, :, cols] = now
            if f == 1:
                image[:, cols] = first_image[:, cols] + correlation(next_fields[0, :, cols], now)

    for f in range(2):
        sent_cols(f, sa1.at[f], f)
        sent(sa3.at[f], 3 + f)
    for src, sem in ((sa2, 2), (sa4, 5)):
        sent(src.at[pl.ds(0, N - ROWS)], sem)


def per_device(flight_fields, top_fields, slowness, ref_slowness, flight_blocks, top_block):
    hbm = pl.BlockSpec(memory_space=pltpu.HBM)
    smem = pl.BlockSpec(memory_space=pltpu.SMEM)
    vmem = pl.BlockSpec(memory_space=pltpu.VMEM)
    pairs = (2, 2 * ROWS, N)
    planes = (2, CHIPS, ROWS, 128)
    stacked, flipped = make_tables()
    image, after_second = pl.pallas_call(
        kernel,
        out_shape=(jax.ShapeDtypeStruct((ROWS, N), f32), jax.ShapeDtypeStruct(pairs, bf16)),
        in_specs=[hbm] * 6 + [smem] * 2,
        out_specs=(vmem, vmem),
        scratch_shapes=[
            pltpu.VMEM((4, 2 * Q, Q), bf16),
            pltpu.VMEM((4, 2 * Q, Q), bf16),
            pltpu.VMEM(pairs, bf16),
            pltpu.VMEM(pairs, bf16),
            pltpu.VMEM((ROWS, N), f32),
            pltpu.VMEM((ROWS, N), f32),
            pltpu.VMEM((N, 128), bf16),
            pltpu.VMEM((N, 128), bf16),
            pltpu.VMEM(planes, bf16),
            pltpu.VMEM(planes, bf16),
            pltpu.VMEM(planes, bf16),
            pltpu.VMEM((N, 128), bf16),
            pltpu.VMEM(planes, bf16),
            pltpu.VMEM((N, 128), bf16),
            pltpu.VMEM(pairs, bf16),
            pltpu.VMEM((4, Q, 128), bf16),
            pltpu.VMEM((4, Q, 128), bf16),
            pltpu.VMEM((4, 2 * Q, 128), f32),
            pltpu.VMEM((2, N, 128), f32),
            pltpu.VMEM((2, N, 128), f32),
            pltpu.VMEM((2, ROWS, N), f32),
            pltpu.VMEM((2, ROWS, N), f32),
            pltpu.SMEM((DEPTH,), jnp.int32),
            pltpu.SemaphoreType.DMA((6,)),
            pltpu.SemaphoreType.DMA((6,)),
            pltpu.SemaphoreType.DMA((6,)),
            pltpu.SemaphoreType.REGULAR,
        ],
        compiler_params=pltpu.CompilerParams(collective_id=0, has_side_effects=True, vmem_limit_bytes=48 << 20),
        name="continuation",
    )(
        *(
            pltpu.with_memory_space_constraint(value, pltpu.HBM)
            for value in (
                jnp.asarray(stacked),
                jnp.asarray(flipped),
                flight_fields.reshape(pairs),
                top_fields.reshape(pairs),
                slowness.reshape(ROWS, N),
                flight_blocks,
            )
        ),
        ref_slowness,
        top_block,
    )
    return image[None], after_second.reshape(1, 2, 2, ROWS, N)


def solution(mesh):
    placed = (
        P("depth", None, None, "trans", None),
        P(None, None, "trans", None),
        P("depth", "trans", None),
        P("depth"),
        P(),
        P(),
    )
    return jax.shard_map(
        per_device,
        mesh=mesh,
        in_specs=placed,
        out_specs=(P("depth", "trans", None), P("depth", None, None, "trans", None)),
        check_vma=False,
    )
```

```python
import math

import jax
import jax.numpy as jnp
import ml_dtypes
import numpy as np
from jax import lax
from jax.experimental import pallas as pl
from jax.experimental.pallas import tpu as pltpu
from jax.sharding import PartitionSpec as P

MESH = pl.DeviceIdType.MESH
N = 1024
NFREQ = 256
DEPTH = 16
TRANS = 32
CHIPS = TRANS // 2
ROWS = N // TRANS
HALF = N // CHIPS
Q = N // 4
BLOCK = 64
omega_top = 4.0
step_length = 0.5
f32 = jnp.float32
bf16 = jnp.bfloat16


def make_tables():
    k = 4 * np.arange(Q)[None, :, None] + np.arange(4)[:, None, None]
    angles = (k * np.arange(Q)[None, None, :] % N) * (2.0 * math.pi / N)
    parts = np.stack([np.cos(angles), np.sin(angles)], axis=1) / math.sqrt(N)
    stacked = parts.reshape(4, 2 * Q, Q)
    flipped = parts.transpose(0, 1, 3, 2).reshape(4, 2 * Q, Q)
    return stacked.astype(ml_dtypes.bfloat16), flipped.astype(ml_dtypes.bfloat16)


def sine(x):
    y = x * x
    p = 1.0 / 355687428096000.0
    for factorial in (1307674368000.0, 6227020800.0, 39916800.0, 362880.0, 5040.0, 120.0, 6.0, 1.0):
        p = 1.0 / factorial - y * p
    return x * p


def cosine(x):
    y = x * x
    p = 1.0 / 20922789888000.0
    for factorial in (87178291200.0, 479001600.0, 3628800.0, 40320.0, 720.0, 24.0, 2.0, 1.0):
        p = 1.0 / factorial - y * p
    return p


def wavenumber(positions):
    signed = jnp.where(positions < N // 2, positions, positions - N)
    return signed.astype(f32) * (2.0 * math.pi / N)


def low_lanes():
    return lax.broadcasted_iota(jnp.int32, (1, 128), 1) < 64


def times_i(v):
    return pltpu.roll(v, 64, 1) * jnp.where(low_lanes(), -1.0, 1.0)


def turned(v):
    return jnp.concatenate([-v[ROWS:], v[:ROWS]], axis=0)


def y_forward(u, tables, dst):
    low = low_lanes()
    u0, u1, u2, u3 = (u[:, Q * j : Q * (j + 1)].astype(f32) for j in range(4))
    a, b, c, d = u0 + u2, u1 + u3, u0 - u2, turned(u1 - u3)
    for r, v in enumerate((a + b, c - d, a - b, c + d)):
        v = v.astype(bf16)
        left = jnp.concatenate([v, -turned(v)], axis=1)
        out = jnp.dot(left, tables[r], preferred_element_type=f32)
        for h in range(2):
            re = out[:ROWS, 128 * h : 128 * (h + 1)]
            im = out[ROWS:, 128 * h : 128 * (h + 1)]
            q = 4 * r + 2 * h
            dst[q] = jnp.where(low, re, pltpu.roll(im, 64, 1)).astype(bf16)
            dst[q + 1] = jnp.where(low, pltpu.roll(re, 64, 1), im).astype(bf16)


def y_inverse(src, tables):
    low = low_lanes()
    w = []
    for r in range(4):
        re, im = [], []
        for h in range(2):
            even = src[4 * r + 2 * h].astype(f32)
            odd = src[4 * r + 2 * h + 1].astype(f32)
            re.append(jnp.where(low, even, pltpu.roll(odd, 64, 1)))
            im.append(jnp.where(low, pltpu.roll(even, 64, 1), odd))
        v = jnp.concatenate([jnp.concatenate(re, axis=1), jnp.concatenate(im, axis=1)], axis=0).astype(bf16)
        left = jnp.concatenate([v, turned(v)], axis=1)
        w.append(jnp.dot(left, tables[r], preferred_element_type=f32))
    a, b, c, d = w[0] + w[2], w[1] + w[3], w[0] - w[2], turned(w[1] - w[3])
    return a + b, c + d, a - b, c - d


def x_stage(src, dst, tables, flipped, spec_c, spec_s, v_ref, g_ref, w_ref):
    for i in range(Q // BLOCK):
        rows = slice(BLOCK * i, BLOCK * (i + 1))
        u0, u1, u2, u3 = (src[Q * j + BLOCK * i : Q * j + BLOCK * (i + 1)].astype(f32) for j in range(4))
        a, b, c, d = u0 + u2, u1 + u3, u0 - u2, times_i(u1 - u3)
        for r, v in enumerate((a + b, c - d, a - b, c + d)):
            v_ref[r, rows] = v.astype(bf16)
    for r in range(4):
        out = jnp.dot(tables[r], v_ref[r], preferred_element_type=f32)
        p, q = out[:Q], out[Q:]
        cosines, sines = spec_c[Q * r : Q * (r + 1)], spec_s[Q * r : Q * (r + 1)]
        g_ref[r] = (p * cosines + q * sines + times_i(p * sines - q * cosines)).astype(bf16)
    for r in range(4):
        w_ref[r] = jnp.dot(flipped[r], g_ref[r], preferred_element_type=f32)
    for i in range(Q // BLOCK):
        p = [w_ref[r, BLOCK * i : BLOCK * (i + 1)] for r in range(4)]
        q = [w_ref[r, Q + BLOCK * i : Q + BLOCK * (i + 1)] for r in range(4)]
        pa, pb, pc, pd = p[0] + p[2], p[1] + p[3], p[0] - p[2], p[1] - p[3]
        qa, qb, qc, qd = q[0] + q[2], q[1] + q[3], q[0] - q[2], q[1] - q[3]
        pairs = ((pa + pb, qa + qb), (pc - qd, qc + pd), (pa - pb, qa - qb), (pc + qd, qc - pd))
        for j, (re, im) in enumerate(pairs):
            dst[Q * j + BLOCK * i : Q * j + BLOCK * (i + 1)] = (re + times_i(im)).astype(bf16)


def spectral(angular, reference_s, chip, sign, spec_c, spec_s):
    square = (angular * reference_s) * (angular * reference_s)
    lanes = lax.broadcasted_iota(jnp.int32, (1, 128), 1)
    wave_y = wavenumber(4 * (HALF * lax.rem(chip, 4) + lax.rem(lanes, 64)) + chip // 4)

    @pl.loop(0, N // BLOCK)
    def _(i):
        start = pl.multiple_of(i * BLOCK, BLOCK)
        r, first = i // (Q // BLOCK), lax.rem(i, Q // BLOCK) * BLOCK
        wave_x = wavenumber(4 * (first + lax.broadcasted_iota(jnp.int32, (BLOCK, 1), 0)) + r)
        quad = square - wave_x * wave_x - wave_y * wave_y
        size = jnp.sqrt(jnp.abs(quad)) * step_length
        damping = jnp.where(quad < 0.0, jnp.exp(-size), 1.0)
        travel = jnp.where(quad < 0.0, 0.0, size)
        spec_c[pl.ds(start, BLOCK)] = damping * cosine(travel)
        spec_s[pl.ds(start, BLOCK)] = damping * sine(travel) * sign


def rotations(angular, reference_s, slow, rot_c, rot_s):
    @pl.loop(0, 4)
    def _(j):
        cols = pl.ds(pl.multiple_of(j * Q, Q), Q)
        rotation = angular * (slow[:, cols] - reference_s) * step_length
        rot_c[:, cols] = cosine(rotation)
        rot_s[:, cols] = sine(rotation)


def rotated(v, cosines, sines):
    re, im = v[:ROWS], v[ROWS:]
    return jnp.concatenate([re * cosines - im * sines, re * sines + im * cosines], axis=0).astype(bf16)


def correlation(source, receiver):
    source, receiver = source.astype(f32), receiver.astype(f32)
    return source[:ROWS] * receiver[:ROWS] + source[ROWS:] * receiver[ROWS:]


def kernel(
    tables_hbm, flipped_hbm, flight_hbm, top_hbm, slow_hbm, blocks_hbm, ref_s, top_block,
    image, next_fields,
    tables, flipped, flight, top, slow, first_image,
    d1, d3, e2, e4, sa1, sa2, sa3, sa4, step1,
    v_ref, g_ref, w_ref, spec_c, spec_s, rot_c, rot_s,
    flight_blocks, load_sem, send_sem, recv_sem, entered,
):
    s = lax.axis_index("depth")
    t = lax.axis_index("trans")
    chip, core = t // 2, lax.rem(t, 2)
    below, above = lax.rem(s + 1, DEPTH), lax.rem(s + DEPTH - 1, DEPTH)

    loads = [
        pltpu.make_async_copy(src, dst, load_sem.at[i])
        for i, (src, dst) in enumerate(
            ((flight_hbm, flight), (flipped_hbm, flipped), (slow_hbm, slow), (tables_hbm, tables), (top_hbm, top), (blocks_hbm, flight_blocks))
        )
    ]
    for load in loads[:2]:
        load.start()

    barrier = pltpu.get_barrier_semaphore()

    @pl.loop(1, TRANS)
    def _(i):
        pl.semaphore_signal(barrier, inc=1, device_id=(s, lax.rem(t + i, TRANS)), device_id_type=MESH)

    for neighbour in (below, above):
        pl.semaphore_signal(barrier, inc=1, device_id=(neighbour, t), device_id_type=MESH)

    for load in loads[2:]:
        load.start()

    def remote(src, dst, sem_s, sem_r, dd, tt):
        pltpu.make_async_remote_copy(
            src_ref=src, dst_ref=dst, send_sem=send_sem.at[sem_s], recv_sem=recv_sem.at[sem_r],
            device_id=(dd, tt), device_id_type=MESH,
        ).start()

    def nth_chip(j):
        half, i = j // 8, lax.rem(j, 8)
        odd = lax.rem(half + chip, 2)
        way = 1 - 2 * lax.rem(i, 2)
        offset = 8 + (1 - odd) * way * 2 * ((i + 1) // 2) - odd * way * (1 + 2 * (i // 2))
        return lax.rem(chip + offset, CHIPS)

    place = pl.ds(pl.multiple_of(t * ROWS, ROWS), ROWS)

    def send_cols(f, src, dst, sem_s, sem_r):
        @pl.loop(0, CHIPS)
        def _(j):
            q = nth_chip(j)

            @pl.when(q != chip)
            def _():
                remote(src.at[q], dst.at[place], sem_s, sem_r, s, 2 * q + f)

        @pl.when(core == f)
        def _():
            pltpu.make_async_copy(src.at[chip], dst.at[place], recv_sem.at[sem_r]).start()

        @pl.when(core != f)
        def _():
            remote(src.at[chip], dst.at[place], sem_s, sem_r, s, 2 * chip + f)

    def sent_cols(f, src, sem_s):
        @pl.when(core == f)
        def _():
            part = src.at[pl.ds(0, CHIPS - 1)]
            pltpu.make_async_copy(part, part, send_sem.at[sem_s]).wait()

        @pl.when(core != f)
        def _():
            sent(src, sem_s)

    def send_below(f, src, dst, sem_s, sem_r):
        @pl.loop(0, CHIPS)
        def _(j):
            q = nth_chip(j)
            remote(src.at[q], dst.at[place], sem_s, sem_r, below, 2 * q + f)

    def send_rows(src, dst, sem_s, sem_r, early):
        def to_chip(q):
            for c in range(2):
                p = 2 * q + c
                rows = pl.ds(pl.multiple_of(p * ROWS, ROWS), ROWS)
                remote(src.at[rows], dst.at[core, chip], sem_s, sem_r + core, s, p)

        if early:

            @pl.loop(0, early)
            def _(q):
                @pl.when(q != chip)
                def _():
                    to_chip(q)

        @pl.loop(0, CHIPS)
        def _(j):
            q = nth_chip(j)

            @pl.when(jnp.logical_and(q != chip, q >= early))
            def _():
                to_chip(q)

        pltpu.make_async_copy(src.at[place], dst.at[core, chip], recv_sem.at[sem_r + core]).start()
        p = 2 * chip + 1 - core
        rows = pl.ds(pl.multiple_of(p * ROWS, ROWS), ROWS)
        remote(src.at[rows], dst.at[core, chip], sem_s, sem_r + core, s, p)

    def sent(src, sem_s):
        pltpu.make_async_copy(src, src, send_sem.at[sem_s]).wait()

    def arrived(dst, sem_r):
        pltpu.make_async_copy(dst, dst, recv_sem.at[sem_r]).wait()

    loads[0].wait()
    loads[1].wait()
    y_forward(flight[0], flipped, sa1.at[0])
    pl.semaphore_wait(barrier, TRANS + 1)
    pl.semaphore_signal(entered, inc=1, device_id=(above, t), device_id_type=MESH)
    send_cols(0, sa1.at[0], d1, 0, 0)
    y_forward(flight[1], flipped, sa1.at[1])
    send_cols(1, sa1.at[1], d1, 1, 0)
    for load in loads[2:]:
        load.wait()
    pl.semaphore_wait(entered, 1)

    @pl.when(s == DEPTH - 1)
    def _():
        for f in range(2):
            y_forward(top[f], flipped, sa3.at[f])
            send_below(f, sa3.at[f], d3, 3 + f, 3)

    reference_s = ref_s[0]
    sign = jnp.where(core == 0, 1.0, -1.0)
    first = flight_blocks[s]
    second = jnp.where(s == 0, top_block[0], flight_blocks[jnp.maximum(s - 1, 0)])
    for step, block in enumerate((first, second)):
        angular = omega_top * (block.astype(f32) + 1.0) / NFREQ
        spectral(angular, reference_s, chip, sign, spec_c.at[step], spec_s.at[step])
        rotations(angular, reference_s, slow, rot_c.at[step], rot_s.at[step])
    arrived(d1, 0)
    x_stage(d1, sa2, tables, flipped, spec_c.at[0], spec_s.at[0], v_ref, g_ref, w_ref)
    send_rows(sa2, e2, 2, 1, 0)
    for f in range(2):
        arrived(e2.at[f], 1 + f)
        for j, v in enumerate(y_inverse(e2.at[f], tables)):
            cols = slice(Q * j, Q * (j + 1))
            now = rotated(v, rot_c[0, :, cols], rot_s[0, :, cols] * (1.0 - 2.0 * f))
            step1[f, :, cols] = now
            if f == 1:
                first_image[:, cols] = correlation(step1[0, :, cols], now)

        @pl.when(s < DEPTH - 1)
        def _():
            y_forward(step1[f], flipped, sa3.at[f])
            send_below(f, sa3.at[f], d3, 3 + f, 3)


    arrived(d3, 3)
    x_stage(d3, sa4, tables, flipped, spec_c.at[1], spec_s.at[1], v_ref, g_ref, w_ref)
    send_rows(sa4, e4, 5, 4, 2)
    for f in range(2):
        arrived(e4.at[f], 4 + f)
        for j, v in enumerate(y_inverse(e4.at[f], tables)):
            cols = slice(Q * j, Q * (j + 1))
            now = rotated(v, rot_c[1, :, cols], rot_s[1, :, cols] * (1.0 - 2.0 * f))
            next_fields[f, :, cols] = now
            if f == 1:
                image[:, cols] = first_image[:, cols] + correlation(next_fields[0, :, cols], now)

    for f in range(2):
        sent_cols(f, sa1.at[f], f)
        sent(sa3.at[f], 3 + f)
    for src, sem in ((sa2, 2), (sa4, 5)):
        sent(src.at[pl.ds(0, N - ROWS)], sem)


def per_device(flight_fields, top_fields, slowness, ref_slowness, flight_blocks, top_block):
    hbm = pl.BlockSpec(memory_space=pltpu.HBM)
    smem = pl.BlockSpec(memory_space=pltpu.SMEM)
    vmem = pl.BlockSpec(memory_space=pltpu.VMEM)
    pairs = (2, 2 * ROWS, N)
    planes = (2, CHIPS, ROWS, 128)
    stacked, flipped = make_tables()
    image, after_second = pl.pallas_call(
        kernel,
        out_shape=(jax.ShapeDtypeStruct((ROWS, N), f32), jax.ShapeDtypeStruct(pairs, bf16)),
        in_specs=[hbm] * 6 + [smem] * 2,
        out_specs=(vmem, vmem),
        scratch_shapes=[
            pltpu.VMEM((4, 2 * Q, Q), bf16),
            pltpu.VMEM((4, 2 * Q, Q), bf16),
            pltpu.VMEM(pairs, bf16),
            pltpu.VMEM(pairs, bf16),
            pltpu.VMEM((ROWS, N), f32),
            pltpu.VMEM((ROWS, N), f32),
            pltpu.VMEM((N, 128), bf16),
            pltpu.VMEM((N, 128), bf16),
            pltpu.VMEM(planes, bf16),
            pltpu.VMEM(planes, bf16),
            pltpu.VMEM(planes, bf16),
            pltpu.VMEM((N, 128), bf16),
            pltpu.VMEM(planes, bf16),
            pltpu.VMEM((N, 128), bf16),
            pltpu.VMEM(pairs, bf16),
            pltpu.VMEM((4, Q, 128), bf16),
            pltpu.VMEM((4, Q, 128), bf16),
            pltpu.VMEM((4, 2 * Q, 128), f32),
            pltpu.VMEM((2, N, 128), f32),
            pltpu.VMEM((2, N, 128), f32),
            pltpu.VMEM((2, ROWS, N), f32),
            pltpu.VMEM((2, ROWS, N), f32),
            pltpu.SMEM((DEPTH,), jnp.int32),
            pltpu.SemaphoreType.DMA((6,)),
            pltpu.SemaphoreType.DMA((6,)),
            pltpu.SemaphoreType.DMA((6,)),
            pltpu.SemaphoreType.REGULAR,
        ],
        compiler_params=pltpu.CompilerParams(collective_id=0, has_side_effects=True, vmem_limit_bytes=48 << 20),
        name="continuation",
    )(
        *(
            pltpu.with_memory_space_constraint(value, pltpu.HBM)
            for value in (
                jnp.asarray(stacked),
                jnp.asarray(flipped),
                flight_fields.reshape(pairs),
                top_fields.reshape(pairs),
                slowness.reshape(ROWS, N),
                flight_blocks,
            )
        ),
        ref_slowness,
        top_block,
    )
    return image[None], after_second.reshape(1, 2, 2, ROWS, N)


def solution(mesh):
    placed = (
        P("depth", None, None, "trans", None),
        P(None, None, "trans", None),
        P("depth", "trans", None),
        P("depth"),
        P(),
        P(),
    )
    return jax.shard_map(
        per_device,
        mesh=mesh,
        in_specs=placed,
        out_specs=(P("depth", "trans", None), P("depth", None, None, "trans", None)),
        check_vma=False,
    )
```

```python
import math

import jax
import jax.numpy as jnp
import ml_dtypes
import numpy as np
from jax import lax
from jax.experimental import pallas as pl
from jax.experimental.pallas import tpu as pltpu
from jax.sharding import PartitionSpec as P

MESH = pl.DeviceIdType.MESH
N = 1024
NFREQ = 256
DEPTH = 16
TRANS = 32
CHIPS = TRANS // 2
ROWS = N // TRANS
HALF = N // CHIPS
Q = N // 4
BLOCK = 64
omega_top = 4.0
step_length = 0.5
f32 = jnp.float32
bf16 = jnp.bfloat16


def make_tables():
    k = 4 * np.arange(Q)[None, :, None] + np.arange(4)[:, None, None]
    angles = (k * np.arange(Q)[None, None, :] % N) * (2.0 * math.pi / N)
    parts = np.stack([np.cos(angles), np.sin(angles)], axis=1) / math.sqrt(N)
    stacked = parts.reshape(4, 2 * Q, Q)
    flipped = parts.transpose(0, 1, 3, 2).reshape(4, 2 * Q, Q)
    return stacked.astype(ml_dtypes.bfloat16), flipped.astype(ml_dtypes.bfloat16)


def sine(x):
    y = x * x
    p = 1.0 / 355687428096000.0
    for factorial in (1307674368000.0, 6227020800.0, 39916800.0, 362880.0, 5040.0, 120.0, 6.0, 1.0):
        p = 1.0 / factorial - y * p
    return x * p


def cosine(x):
    y = x * x
    p = 1.0 / 20922789888000.0
    for factorial in (87178291200.0, 479001600.0, 3628800.0, 40320.0, 720.0, 24.0, 2.0, 1.0):
        p = 1.0 / factorial - y * p
    return p


def wavenumber(positions):
    signed = jnp.where(positions < N // 2, positions, positions - N)
    return signed.astype(f32) * (2.0 * math.pi / N)


def low_lanes():
    return lax.broadcasted_iota(jnp.int32, (1, 128), 1) < 64


def times_i(v):
    return pltpu.roll(v, 64, 1) * jnp.where(low_lanes(), -1.0, 1.0)


def turned(v):
    return jnp.concatenate([-v[ROWS:], v[:ROWS]], axis=0)


def y_forward(u, tables, dst):
    low = low_lanes()
    u0, u1, u2, u3 = (u[:, Q * j : Q * (j + 1)].astype(f32) for j in range(4))
    a, b, c, d = u0 + u2, u1 + u3, u0 - u2, turned(u1 - u3)
    for r, v in enumerate((a + b, c - d, a - b, c + d)):
        v = v.astype(bf16)
        left = jnp.concatenate([v, -turned(v)], axis=1)
        out = jnp.dot(left, tables[r], preferred_element_type=f32)
        for h in range(2):
            re = out[:ROWS, 128 * h : 128 * (h + 1)]
            im = out[ROWS:, 128 * h : 128 * (h + 1)]
            q = 4 * r + 2 * h
            dst[q] = jnp.where(low, re, pltpu.roll(im, 64, 1)).astype(bf16)
            dst[q + 1] = jnp.where(low, pltpu.roll(re, 64, 1), im).astype(bf16)


def y_inverse(src, tables):
    low = low_lanes()
    w = []
    for r in range(4):
        re, im = [], []
        for h in range(2):
            even = src[4 * r + 2 * h].astype(f32)
            odd = src[4 * r + 2 * h + 1].astype(f32)
            re.append(jnp.where(low, even, pltpu.roll(odd, 64, 1)))
            im.append(jnp.where(low, pltpu.roll(even, 64, 1), odd))
        v = jnp.concatenate([jnp.concatenate(re, axis=1), jnp.concatenate(im, axis=1)], axis=0).astype(bf16)
        left = jnp.concatenate([v, turned(v)], axis=1)
        w.append(jnp.dot(left, tables[r], preferred_element_type=f32))
    a, b, c, d = w[0] + w[2], w[1] + w[3], w[0] - w[2], turned(w[1] - w[3])
    return a + b, c + d, a - b, c - d


def x_stage(src, dst, tables, flipped, spec_c, spec_s, v_ref, g_ref, w_ref):
    place = {r: slice(128 * n, 128 * (n + 1)) for n, r in enumerate((0, 2, 1, 3))}
    products = ((0, slice(0, 128)), (2, slice(128, 256)), (1, slice(256, 512)))
    for i in range(Q // BLOCK):
        rows = slice(BLOCK * i, BLOCK * (i + 1))
        u0, u1, u2, u3 = (src[Q * j + BLOCK * i : Q * j + BLOCK * (i + 1)].astype(f32) for j in range(4))
        a, b, c, d = u0 + u2, u1 + u3, u0 - u2, times_i(u1 - u3)
        for r, v in enumerate((a + b, c - d, a - b, c + d)):
            v_ref[rows, place[r]] = v.astype(bf16)
    for r, cols in products:
        out = jnp.dot(tables[r], v_ref[:, cols], preferred_element_type=f32)
        cosines, sines = spec_c[Q * r : Q * (r + 1)], spec_s[Q * r : Q * (r + 1)]
        p, q = out[:Q, :128], out[Q:, :128]
        g_ref[:, place[r]] = (p * cosines + q * sines + times_i(p * sines - q * cosines)).astype(bf16)
        if r == 1:
            p, q = out[:Q, 128:], out[Q:, 128:]
            g_ref[:, place[3]] = (p * cosines - q * sines + times_i(p * sines + q * cosines)).astype(bf16)
    for r, cols in products:
        w_ref[:, cols] = jnp.dot(flipped[r], g_ref[:, cols], preferred_element_type=f32)
    for i in range(Q // BLOCK):
        p = [w_ref[BLOCK * i : BLOCK * (i + 1), place[r]] for r in range(4)]
        q = [w_ref[Q + BLOCK * i : Q + BLOCK * (i + 1), place[r]] for r in range(4)]
        pa, pb, pc, pd = p[0] + p[2], p[1] + p[3], p[0] - p[2], p[1] - p[3]
        qa, qb, qc, qd = q[0] + q[2], q[1] - q[3], q[0] - q[2], q[1] + q[3]
        pairs = ((pa + pb, qa + qb), (pc - qd, qc + pd), (pa - pb, qa - qb), (pc + qd, qc - pd))
        for j, (re, im) in enumerate(pairs):
            dst[Q * j + BLOCK * i : Q * j + BLOCK * (i + 1)] = (re + times_i(im)).astype(bf16)


def spectral(angular, reference_s, chip, sign, spec_c, spec_s):
    square = (angular * reference_s) * (angular * reference_s)
    lanes = lax.broadcasted_iota(jnp.int32, (1, 128), 1)
    wave_y = wavenumber(4 * (HALF * lax.rem(chip, 4) + lax.rem(lanes, 64)) + chip // 4)

    @pl.loop(0, 3 * Q // BLOCK)
    def _(i):
        start = pl.multiple_of(i * BLOCK, BLOCK)
        r, first = i // (Q // BLOCK), lax.rem(i, Q // BLOCK) * BLOCK
        wave_x = wavenumber(4 * (first + lax.broadcasted_iota(jnp.int32, (BLOCK, 1), 0)) + r)
        quad = square - wave_x * wave_x - wave_y * wave_y
        size = jnp.sqrt(jnp.abs(quad)) * step_length
        damping = jnp.where(quad < 0.0, jnp.exp(-size), 1.0)
        travel = jnp.where(quad < 0.0, 0.0, size)
        spec_c[pl.ds(start, BLOCK)] = damping * cosine(travel)
        spec_s[pl.ds(start, BLOCK)] = damping * sine(travel) * sign


def rotations(angular, reference_s, slow, rot_c, rot_s):
    @pl.loop(0, 4)
    def _(j):
        cols = pl.ds(pl.multiple_of(j * Q, Q), Q)
        rotation = angular * (slow[:, cols] - reference_s) * step_length
        rot_c[:, cols] = cosine(rotation)
        rot_s[:, cols] = sine(rotation)


def rotated(v, cosines, sines):
    re, im = v[:ROWS], v[ROWS:]
    return jnp.concatenate([re * cosines - im * sines, re * sines + im * cosines], axis=0).astype(bf16)


def correlation(source, receiver):
    source, receiver = source.astype(f32), receiver.astype(f32)
    return source[:ROWS] * receiver[:ROWS] + source[ROWS:] * receiver[ROWS:]


def kernel(
    tables_hbm, flipped_hbm, flight_hbm, top_hbm, slow_hbm, blocks_hbm, ref_s, top_block,
    image, next_fields,
    tables, flipped, flight, top, slow, first_image,
    d1, d3, e2, e4, sa1, sa2, sa3, sa4, step1,
    v_ref, g_ref, w_ref, spec_c, spec_s, rot_c, rot_s,
    flight_blocks, load_sem, send_sem, recv_sem, entered,
):
    s = lax.axis_index("depth")
    t = lax.axis_index("trans")
    chip, core = t // 2, lax.rem(t, 2)
    below, above = lax.rem(s + 1, DEPTH), lax.rem(s + DEPTH - 1, DEPTH)

    loads = [
        pltpu.make_async_copy(src, dst, load_sem.at[i])
        for i, (src, dst) in enumerate(
            ((flight_hbm, flight), (flipped_hbm, flipped), (slow_hbm, slow), (tables_hbm, tables), (top_hbm, top), (blocks_hbm, flight_blocks))
        )
    ]
    for load in loads[:2]:
        load.start()

    barrier = pltpu.get_barrier_semaphore()

    for neighbour in (below, above):
        pl.semaphore_signal(barrier, inc=1, device_id=(neighbour, t), device_id_type=MESH)

    @pl.loop(1, TRANS)
    def _(i):
        pl.semaphore_signal(barrier, inc=1, device_id=(s, lax.rem(t + TRANS - i, TRANS)), device_id_type=MESH)

    for load in loads[2:]:
        load.start()

    def remote(src, dst, sem_s, sem_r, dd, tt):
        pltpu.make_async_remote_copy(
            src_ref=src, dst_ref=dst, send_sem=send_sem.at[sem_s], recv_sem=recv_sem.at[sem_r],
            device_id=(dd, tt), device_id_type=MESH,
        ).start()

    def nth_chip(j):
        half, i = j // 8, lax.rem(j, 8)
        odd = lax.rem(half + chip, 2)
        way = 1 - 2 * lax.rem(i, 2)
        offset = 8 + (1 - odd) * way * 2 * ((i + 1) // 2) - odd * way * (1 + 2 * (i // 2))
        return lax.rem(chip + offset, CHIPS)

    place = pl.ds(pl.multiple_of(t * ROWS, ROWS), ROWS)

    def send_cols(f, src, dst, sem_s, sem_r):
        @pl.loop(0, CHIPS)
        def _(j):
            q = nth_chip(j)

            @pl.when(q != chip)
            def _():
                remote(src.at[q], dst.at[place], sem_s, sem_r, s, 2 * q + f)

        @pl.when(core == f)
        def _():
            pltpu.make_async_copy(src.at[chip], dst.at[place], recv_sem.at[sem_r]).start()

        @pl.when(core != f)
        def _():
            remote(src.at[chip], dst.at[place], sem_s, sem_r, s, 2 * chip + f)

    def sent_cols(f, src, sem_s):
        @pl.when(core == f)
        def _():
            part = src.at[pl.ds(0, CHIPS - 1)]
            pltpu.make_async_copy(part, part, send_sem.at[sem_s]).wait()

        @pl.when(core != f)
        def _():
            sent(src, sem_s)

    def send_below(f, src, dst, sem_s, sem_r):
        @pl.loop(0, CHIPS)
        def _(j):
            q = nth_chip(j)
            remote(src.at[q], dst.at[place], sem_s, sem_r, below, 2 * q + f)

    def send_rows(src, dst, sem_s, sem_r, early):
        def to_chip(q):
            for c in range(2):
                p = 2 * q + c
                rows = pl.ds(pl.multiple_of(p * ROWS, ROWS), ROWS)
                remote(src.at[rows], dst.at[core, chip], sem_s, sem_r + core, s, p)

        if early:

            @pl.loop(0, early)
            def _(q):
                @pl.when(q != chip)
                def _():
                    to_chip(q)

        @pl.loop(0, CHIPS)
        def _(j):
            q = nth_chip(j)

            @pl.when(jnp.logical_and(q != chip, q >= early))
            def _():
                to_chip(q)

        pltpu.make_async_copy(src.at[place], dst.at[core, chip], recv_sem.at[sem_r + core]).start()
        p = 2 * chip + 1 - core
        rows = pl.ds(pl.multiple_of(p * ROWS, ROWS), ROWS)
        remote(src.at[rows], dst.at[core, chip], sem_s, sem_r + core, s, p)

    def sent(src, sem_s):
        pltpu.make_async_copy(src, src, send_sem.at[sem_s]).wait()

    def arrived(dst, sem_r):
        pltpu.make_async_copy(dst, dst, recv_sem.at[sem_r]).wait()

    loads[0].wait()
    loads[1].wait()
    y_forward(flight[0], flipped, sa1.at[0])
    pl.semaphore_wait(barrier, TRANS + 1)
    pl.semaphore_signal(entered, inc=1, device_id=(above, t), device_id_type=MESH)
    send_cols(0, sa1.at[0], d1, 0, 0)
    y_forward(flight[1], flipped, sa1.at[1])
    send_cols(1, sa1.at[1], d1, 1, 0)
    for load in loads[2:]:
        load.wait()
    pl.semaphore_wait(entered, 1)

    @pl.when(s == DEPTH - 1)
    def _():
        for f in range(2):
            y_forward(top[f], flipped, sa3.at[f])
            send_below(f, sa3.at[f], d3, 3 + f, 3)

    reference_s = ref_s[0]
    sign = jnp.where(core == 0, 1.0, -1.0)
    first = flight_blocks[s]
    second = jnp.where(s == 0, top_block[0], flight_blocks[jnp.maximum(s - 1, 0)])
    for step, block in enumerate((first, second)):
        angular = omega_top * (block.astype(f32) + 1.0) / NFREQ
        spectral(angular, reference_s, chip, sign, spec_c.at[step], spec_s.at[step])
        rotations(angular, reference_s, slow, rot_c.at[step], rot_s.at[step])
    arrived(d1, 0)
    x_stage(d1, sa2, tables, flipped, spec_c.at[0], spec_s.at[0], v_ref, g_ref, w_ref)
    send_rows(sa2, e2, 2, 1, 0)
    for f in range(2):
        arrived(e2.at[f], 1 + f)
        for j, v in enumerate(y_inverse(e2.at[f], tables)):
            cols = slice(Q * j, Q * (j + 1))
            now = rotated(v, rot_c[0, :, cols], rot_s[0, :, cols] * (1.0 - 2.0 * f))
            step1[f, :, cols] = now
            if f == 1:
                first_image[:, cols] = correlation(step1[0, :, cols], now)

        @pl.when(s < DEPTH - 1)
        def _():
            y_forward(step1[f], flipped, sa3.at[f])
            send_below(f, sa3.at[f], d3, 3 + f, 3)


    arrived(d3, 3)
    x_stage(d3, sa4, tables, flipped, spec_c.at[1], spec_s.at[1], v_ref, g_ref, w_ref)
    send_rows(sa4, e4, 5, 4, 2)
    for f in range(2):
        arrived(e4.at[f], 4 + f)
        for j, v in enumerate(y_inverse(e4.at[f], tables)):
            cols = slice(Q * j, Q * (j + 1))
            now = rotated(v, rot_c[1, :, cols], rot_s[1, :, cols] * (1.0 - 2.0 * f))
            next_fields[f, :, cols] = now
            if f == 1:
                image[:, cols] = first_image[:, cols] + correlation(next_fields[0, :, cols], now)

    for f in range(2):
        sent_cols(f, sa1.at[f], f)
        sent(sa3.at[f], 3 + f)
    for src, sem in ((sa2, 2), (sa4, 5)):
        sent(src.at[pl.ds(0, N - ROWS)], sem)


def store(image, fields, image_out, fields_out, sems):
    copies = [pltpu.make_async_copy(image, image_out, sems.at[0]), pltpu.make_async_copy(fields, fields_out, sems.at[1])]
    for copy in copies:
        copy.start()
    for copy in copies:
        copy.wait()


def per_device(flight_fields, top_fields, slowness, ref_slowness, flight_blocks, top_block):
    hbm = pl.BlockSpec(memory_space=pltpu.HBM)
    smem = pl.BlockSpec(memory_space=pltpu.SMEM)
    vmem = pl.BlockSpec(memory_space=pltpu.VMEM)
    pairs = (2, 2 * ROWS, N)
    planes = (2, CHIPS, ROWS, 128)
    stacked, flipped = make_tables()
    image, after_second = pl.pallas_call(
        kernel,
        out_shape=(jax.ShapeDtypeStruct((ROWS, N), f32), jax.ShapeDtypeStruct(pairs, bf16)),
        in_specs=[hbm] * 6 + [smem] * 2,
        out_specs=(vmem, vmem),
        scratch_shapes=[
            pltpu.VMEM((4, 2 * Q, Q), bf16),
            pltpu.VMEM((4, 2 * Q, Q), bf16),
            pltpu.VMEM(pairs, bf16),
            pltpu.VMEM(pairs, bf16),
            pltpu.VMEM((ROWS, N), f32),
            pltpu.VMEM((ROWS, N), f32),
            pltpu.VMEM((N, 128), bf16),
            pltpu.VMEM((N, 128), bf16),
            pltpu.VMEM(planes, bf16),
            pltpu.VMEM(planes, bf16),
            pltpu.VMEM(planes, bf16),
            pltpu.VMEM((N, 128), bf16),
            pltpu.VMEM(planes, bf16),
            pltpu.VMEM((N, 128), bf16),
            pltpu.VMEM(pairs, bf16),
            pltpu.VMEM((Q, 512), bf16),
            pltpu.VMEM((Q, 512), bf16),
            pltpu.VMEM((2 * Q, 512), f32),
            pltpu.VMEM((2, 3 * Q, 128), f32),
            pltpu.VMEM((2, 3 * Q, 128), f32),
            pltpu.VMEM((2, ROWS, N), f32),
            pltpu.VMEM((2, ROWS, N), f32),
            pltpu.SMEM((DEPTH,), jnp.int32),
            pltpu.SemaphoreType.DMA((6,)),
            pltpu.SemaphoreType.DMA((6,)),
            pltpu.SemaphoreType.DMA((6,)),
            pltpu.SemaphoreType.REGULAR,
        ],
        compiler_params=pltpu.CompilerParams(collective_id=0, has_side_effects=True, vmem_limit_bytes=48 << 20),
        name="continuation",
    )(
        *(
            pltpu.with_memory_space_constraint(value, pltpu.HBM)
            for value in (
                jnp.asarray(stacked),
                jnp.asarray(flipped),
                flight_fields.reshape(pairs),
                top_fields.reshape(pairs),
                slowness.reshape(ROWS, N),
                flight_blocks,
            )
        ),
        ref_slowness,
        top_block,
    )
    out = pl.BlockSpec(memory_space=pltpu.HBM)
    image, after_second = pl.pallas_call(
        store,
        out_shape=(jax.ShapeDtypeStruct((ROWS, N), f32), jax.ShapeDtypeStruct(pairs, bf16)),
        in_specs=[vmem, vmem],
        out_specs=(out, out),
        scratch_shapes=[pltpu.SemaphoreType.DMA((2,))],
        compiler_params=pltpu.CompilerParams(vmem_limit_bytes=2 << 20),
        name="store",
    )(image, after_second)
    return image[None], after_second.reshape(1, 2, 2, ROWS, N)


def solution(mesh):
    placed = (
        P("depth", None, None, "trans", None),
        P(None, None, "trans", None),
        P("depth", "trans", None),
        P("depth"),
        P(),
        P(),
    )
    return jax.shard_map(
        per_device,
        mesh=mesh,
        in_specs=placed,
        out_specs=(P("depth", "trans", None), P("depth", None, None, "trans", None)),
        check_vma=False,
    )
```

```python
import math

import jax
import jax.numpy as jnp
import ml_dtypes
import numpy as np
from jax import lax
from jax.experimental import pallas as pl
from jax.experimental.pallas import tpu as pltpu
from jax.sharding import PartitionSpec as P

MESH = pl.DeviceIdType.MESH
N = 1024
NFREQ = 256
DEPTH = 16
TRANS = 32
CHIPS = TRANS // 2
ROWS = N // TRANS
HALF = N // CHIPS
Q = N // 4
BLOCK = 64
omega_top = 4.0
step_length = 0.5
f32 = jnp.float32
bf16 = jnp.bfloat16


def make_tables():
    k = 4 * np.arange(Q)[None, :, None] + np.arange(4)[:, None, None]
    angles = (k * np.arange(Q)[None, None, :] % N) * (2.0 * math.pi / N)
    parts = np.stack([np.cos(angles), np.sin(angles)], axis=1) / math.sqrt(N)
    stacked = parts.reshape(4, 2 * Q, Q)
    flipped = parts.transpose(0, 1, 3, 2).reshape(4, 2 * Q, Q)
    return stacked.astype(ml_dtypes.bfloat16), flipped.astype(ml_dtypes.bfloat16)


def sine(x):
    y = x * x
    p = 1.0 / 355687428096000.0
    for factorial in (1307674368000.0, 6227020800.0, 39916800.0, 362880.0, 5040.0, 120.0, 6.0, 1.0):
        p = 1.0 / factorial - y * p
    return x * p


def cosine(x):
    y = x * x
    p = 1.0 / 20922789888000.0
    for factorial in (87178291200.0, 479001600.0, 3628800.0, 40320.0, 720.0, 24.0, 2.0, 1.0):
        p = 1.0 / factorial - y * p
    return p


def wavenumber(positions):
    signed = jnp.where(positions < N // 2, positions, positions - N)
    return signed.astype(f32) * (2.0 * math.pi / N)


def low_lanes():
    return lax.broadcasted_iota(jnp.int32, (1, 128), 1) < 64


def times_i(v):
    return pltpu.roll(v, 64, 1) * jnp.where(low_lanes(), -1.0, 1.0)


def turned(v):
    return jnp.concatenate([-v[ROWS:], v[:ROWS]], axis=0)


def y_forward(u, tables, dst):
    low = low_lanes()
    u0, u1, u2, u3 = (u[:, Q * j : Q * (j + 1)].astype(f32) for j in range(4))
    a, b, c, d = u0 + u2, u1 + u3, u0 - u2, turned(u1 - u3)
    for r, v in enumerate((a + b, c - d, a - b, c + d)):
        v = v.astype(bf16)
        left = jnp.concatenate([v, -turned(v)], axis=1)
        out = jnp.dot(left, tables[r], preferred_element_type=f32)
        for h in range(2):
            re = out[:ROWS, 128 * h : 128 * (h + 1)]
            im = out[ROWS:, 128 * h : 128 * (h + 1)]
            q = 4 * r + 2 * h
            dst[q] = jnp.where(low, re, pltpu.roll(im, 64, 1)).astype(bf16)
            dst[q + 1] = jnp.where(low, pltpu.roll(re, 64, 1), im).astype(bf16)


def y_inverse(src, tables):
    low = low_lanes()
    w = []
    for r in range(4):
        re, im = [], []
        for h in range(2):
            even = src[4 * r + 2 * h].astype(f32)
            odd = src[4 * r + 2 * h + 1].astype(f32)
            re.append(jnp.where(low, even, pltpu.roll(odd, 64, 1)))
            im.append(jnp.where(low, pltpu.roll(even, 64, 1), odd))
        v = jnp.concatenate([jnp.concatenate(re, axis=1), jnp.concatenate(im, axis=1)], axis=0).astype(bf16)
        left = jnp.concatenate([v, turned(v)], axis=1)
        w.append(jnp.dot(left, tables[r], preferred_element_type=f32))
    a, b, c, d = w[0] + w[2], w[1] + w[3], w[0] - w[2], turned(w[1] - w[3])
    return a + b, c + d, a - b, c - d


def x_stage(src, dst, tables, flipped, spec_c, spec_s, v_ref, g_ref, w_ref):
    place = {r: slice(128 * n, 128 * (n + 1)) for n, r in enumerate((0, 2, 1, 3))}
    products = ((0, slice(0, 128)), (2, slice(128, 256)), (1, slice(256, 512)))
    for i in range(Q // BLOCK):
        rows = slice(BLOCK * i, BLOCK * (i + 1))
        u0, u1, u2, u3 = (src[Q * j + BLOCK * i : Q * j + BLOCK * (i + 1)].astype(f32) for j in range(4))
        a, b, c, d = u0 + u2, u1 + u3, u0 - u2, times_i(u1 - u3)
        for r, v in enumerate((a + b, c - d, a - b, c + d)):
            v_ref[rows, place[r]] = v.astype(bf16)
    for r, cols in products:
        out = jnp.dot(tables[r], v_ref[:, cols], preferred_element_type=f32)
        cosines, sines = spec_c[Q * r : Q * (r + 1)], spec_s[Q * r : Q * (r + 1)]
        p, q = out[:Q, :128], out[Q:, :128]
        g_ref[:, place[r]] = (p * cosines + q * sines + times_i(p * sines - q * cosines)).astype(bf16)
        if r == 1:
            p, q = out[:Q, 128:], out[Q:, 128:]
            g_ref[:, place[3]] = (p * cosines - q * sines + times_i(p * sines + q * cosines)).astype(bf16)
    for r, cols in products:
        w_ref[:, cols] = jnp.dot(flipped[r], g_ref[:, cols], preferred_element_type=f32)
    for i in range(Q // BLOCK):
        p = [w_ref[BLOCK * i : BLOCK * (i + 1), place[r]] for r in range(4)]
        q = [w_ref[Q + BLOCK * i : Q + BLOCK * (i + 1), place[r]] for r in range(4)]
        pa, pb, pc, pd = p[0] + p[2], p[1] + p[3], p[0] - p[2], p[1] - p[3]
        qa, qb, qc, qd = q[0] + q[2], q[1] - q[3], q[0] - q[2], q[1] + q[3]
        pairs = ((pa + pb, qa + qb), (pc - qd, qc + pd), (pa - pb, qa - qb), (pc + qd, qc - pd))
        for j, (re, im) in enumerate(pairs):
            dst[Q * j + BLOCK * i : Q * j + BLOCK * (i + 1)] = (re + times_i(im)).astype(bf16)


def spectral(angular, reference_s, chip, sign, spec_c, spec_s):
    square = (angular * reference_s) * (angular * reference_s)
    lanes = lax.broadcasted_iota(jnp.int32, (1, 128), 1)
    wave_y = wavenumber(4 * (HALF * lax.rem(chip, 4) + lax.rem(lanes, 64)) + chip // 4)

    @pl.loop(0, 3 * Q // BLOCK)
    def _(i):
        start = pl.multiple_of(i * BLOCK, BLOCK)
        r, first = i // (Q // BLOCK), lax.rem(i, Q // BLOCK) * BLOCK
        wave_x = wavenumber(4 * (first + lax.broadcasted_iota(jnp.int32, (BLOCK, 1), 0)) + r)
        quad = square - wave_x * wave_x - wave_y * wave_y
        size = jnp.sqrt(jnp.abs(quad)) * step_length
        damping = jnp.where(quad < 0.0, jnp.exp(-size), 1.0)
        travel = jnp.where(quad < 0.0, 0.0, size)
        spec_c[pl.ds(start, BLOCK)] = damping * cosine(travel)
        spec_s[pl.ds(start, BLOCK)] = damping * sine(travel) * sign


def rotations(angular, reference_s, slow, rot_c, rot_s):
    @pl.loop(0, 4)
    def _(j):
        cols = pl.ds(pl.multiple_of(j * Q, Q), Q)
        rotation = angular * (slow[:, cols] - reference_s) * step_length
        rot_c[:, cols] = cosine(rotation)
        rot_s[:, cols] = sine(rotation)


def rotated(v, cosines, sines):
    re, im = v[:ROWS], v[ROWS:]
    return jnp.concatenate([re * cosines - im * sines, re * sines + im * cosines], axis=0).astype(bf16)


def correlation(source, receiver):
    source, receiver = source.astype(f32), receiver.astype(f32)
    return source[:ROWS] * receiver[:ROWS] + source[ROWS:] * receiver[ROWS:]


def kernel(
    tables_hbm, flipped_hbm, flight_hbm, top_hbm, slow_hbm, blocks_hbm, ref_s, top_block,
    image, next_fields,
    tables, flipped, flight, top, slow, first_image,
    d1, d3, e2, e4, sa1, sa2, sa3, sa4, step1,
    v_ref, g_ref, w_ref, spec_c, spec_s, rot_c, rot_s,
    flight_blocks, load_sem, send_sem, recv_sem, entered,
):
    s = lax.axis_index("depth")
    t = lax.axis_index("trans")
    chip, core = t // 2, lax.rem(t, 2)
    below, above = lax.rem(s + 1, DEPTH), lax.rem(s + DEPTH - 1, DEPTH)

    loads = [
        pltpu.make_async_copy(src, dst, load_sem.at[i])
        for i, (src, dst) in enumerate(
            ((flight_hbm, flight), (flipped_hbm, flipped), (slow_hbm, slow), (tables_hbm, tables), (top_hbm, top), (blocks_hbm, flight_blocks))
        )
    ]
    for load in loads[:2]:
        load.start()

    barrier = pltpu.get_barrier_semaphore()

    for neighbour in (below, above):
        pl.semaphore_signal(barrier, inc=1, device_id=(neighbour, t), device_id_type=MESH)

    @pl.loop(1, TRANS)
    def _(i):
        pl.semaphore_signal(barrier, inc=1, device_id=(s, lax.rem(t + TRANS - i, TRANS)), device_id_type=MESH)

    for load in loads[2:]:
        load.start()

    def remote(src, dst, sem_s, sem_r, dd, tt):
        pltpu.make_async_remote_copy(
            src_ref=src, dst_ref=dst, send_sem=send_sem.at[sem_s], recv_sem=recv_sem.at[sem_r],
            device_id=(dd, tt), device_id_type=MESH,
        ).start()

    def nth_chip(j):
        half, i = j // 8, lax.rem(j, 8)
        odd = lax.rem(half + chip, 2)
        way = 1 - 2 * lax.rem(i, 2)
        offset = 8 + (1 - odd) * way * 2 * ((i + 1) // 2) - odd * way * (1 + 2 * (i // 2))
        return lax.rem(chip + offset, CHIPS)

    place = pl.ds(pl.multiple_of(t * ROWS, ROWS), ROWS)

    def send_cols(f, src, dst, sem_s, sem_r):
        @pl.loop(0, CHIPS)
        def _(j):
            q = nth_chip(j)

            @pl.when(q != chip)
            def _():
                remote(src.at[q], dst.at[place], sem_s, sem_r, s, 2 * q + f)

        @pl.when(core == f)
        def _():
            pltpu.make_async_copy(src.at[chip], dst.at[place], recv_sem.at[sem_r]).start()

        @pl.when(core != f)
        def _():
            remote(src.at[chip], dst.at[place], sem_s, sem_r, s, 2 * chip + f)

    def sent_cols(f, src, sem_s):
        @pl.when(core == f)
        def _():
            part = src.at[pl.ds(0, CHIPS - 1)]
            pltpu.make_async_copy(part, part, send_sem.at[sem_s]).wait()

        @pl.when(core != f)
        def _():
            sent(src, sem_s)

    def send_below(f, src, dst, sem_s, sem_r):
        @pl.loop(0, CHIPS)
        def _(j):
            q = nth_chip(j)
            remote(src.at[q], dst.at[place], sem_s, sem_r, below, 2 * q + f)

    def send_rows(src, dst, sem_s, sem_r, early):
        def to_chip(q):
            for c in range(2):
                p = 2 * q + c
                rows = pl.ds(pl.multiple_of(p * ROWS, ROWS), ROWS)
                remote(src.at[rows], dst.at[core, chip], sem_s, sem_r + core, s, p)

        if early:

            @pl.loop(0, early)
            def _(q):
                @pl.when(q != chip)
                def _():
                    to_chip(q)

        @pl.loop(0, CHIPS)
        def _(j):
            q = nth_chip(j)

            @pl.when(jnp.logical_and(q != chip, q >= early))
            def _():
                to_chip(q)

        pltpu.make_async_copy(src.at[place], dst.at[core, chip], recv_sem.at[sem_r + core]).start()
        p = 2 * chip + 1 - core
        rows = pl.ds(pl.multiple_of(p * ROWS, ROWS), ROWS)
        remote(src.at[rows], dst.at[core, chip], sem_s, sem_r + core, s, p)

    def sent(src, sem_s):
        pltpu.make_async_copy(src, src, send_sem.at[sem_s]).wait()

    def arrived(dst, sem_r):
        pltpu.make_async_copy(dst, dst, recv_sem.at[sem_r]).wait()

    loads[0].wait()
    loads[1].wait()
    y_forward(flight[0], flipped, sa1.at[0])
    pl.semaphore_wait(barrier, TRANS + 1)
    pl.semaphore_signal(entered, inc=1, device_id=(above, t), device_id_type=MESH)
    send_cols(0, sa1.at[0], d1, 0, 0)
    y_forward(flight[1], flipped, sa1.at[1])
    send_cols(1, sa1.at[1], d1, 1, 0)
    for load in loads[2:]:
        load.wait()
    pl.semaphore_wait(entered, 1)

    @pl.when(s == DEPTH - 1)
    def _():
        for f in range(2):
            y_forward(top[f], flipped, sa3.at[f])
            send_below(f, sa3.at[f], d3, 3 + f, 3)

    reference_s = ref_s[0]
    sign = jnp.where(core == 0, 1.0, -1.0)
    first = flight_blocks[s]
    second = jnp.where(s == 0, top_block[0], flight_blocks[jnp.maximum(s - 1, 0)])
    for step, block in enumerate((first, second)):
        angular = omega_top * (block.astype(f32) + 1.0) / NFREQ
        spectral(angular, reference_s, chip, sign, spec_c.at[step], spec_s.at[step])
        rotations(angular, reference_s, slow, rot_c.at[step], rot_s.at[step])
    arrived(d1, 0)
    x_stage(d1, sa2, tables, flipped, spec_c.at[0], spec_s.at[0], v_ref, g_ref, w_ref)
    send_rows(sa2, e2, 2, 1, 0)
    for f in range(2):
        arrived(e2.at[f], 1 + f)
        for j, v in enumerate(y_inverse(e2.at[f], tables)):
            cols = slice(Q * j, Q * (j + 1))
            now = rotated(v, rot_c[0, :, cols], rot_s[0, :, cols] * (1.0 - 2.0 * f))
            step1[f, :, cols] = now
            if f == 1:
                first_image[:, cols] = correlation(step1[0, :, cols], now)

        @pl.when(s < DEPTH - 1)
        def _():
            y_forward(step1[f], flipped, sa3.at[f])
            send_below(f, sa3.at[f], d3, 3 + f, 3)


    arrived(d3, 3)
    x_stage(d3, sa4, tables, flipped, spec_c.at[1], spec_s.at[1], v_ref, g_ref, w_ref)
    send_rows(sa4, e4, 5, 4, 3)
    for f in range(2):
        arrived(e4.at[f], 4 + f)
        for j, v in enumerate(y_inverse(e4.at[f], tables)):
            cols = slice(Q * j, Q * (j + 1))
            now = rotated(v, rot_c[1, :, cols], rot_s[1, :, cols] * (1.0 - 2.0 * f))
            next_fields[f, :, cols] = now
            if f == 1:
                image[:, cols] = first_image[:, cols] + correlation(next_fields[0, :, cols], now)

    for f in range(2):
        sent_cols(f, sa1.at[f], f)
        sent(sa3.at[f], 3 + f)
    for src, sem in ((sa2, 2), (sa4, 5)):
        sent(src.at[pl.ds(0, N - ROWS)], sem)


def store(image, fields, image_out, fields_out, sems):
    copies = [pltpu.make_async_copy(image, image_out, sems.at[0]), pltpu.make_async_copy(fields, fields_out, sems.at[1])]
    for copy in copies:
        copy.start()
    for copy in copies:
        copy.wait()


def per_device(flight_fields, top_fields, slowness, ref_slowness, flight_blocks, top_block):
    hbm = pl.BlockSpec(memory_space=pltpu.HBM)
    smem = pl.BlockSpec(memory_space=pltpu.SMEM)
    vmem = pl.BlockSpec(memory_space=pltpu.VMEM)
    pairs = (2, 2 * ROWS, N)
    planes = (2, CHIPS, ROWS, 128)
    stacked, flipped = make_tables()
    image, after_second = pl.pallas_call(
        kernel,
        out_shape=(jax.ShapeDtypeStruct((ROWS, N), f32), jax.ShapeDtypeStruct(pairs, bf16)),
        in_specs=[hbm] * 6 + [smem] * 2,
        out_specs=(vmem, vmem),
        scratch_shapes=[
            pltpu.VMEM((4, 2 * Q, Q), bf16),
            pltpu.VMEM((4, 2 * Q, Q), bf16),
            pltpu.VMEM(pairs, bf16),
            pltpu.VMEM(pairs, bf16),
            pltpu.VMEM((ROWS, N), f32),
            pltpu.VMEM((ROWS, N), f32),
            pltpu.VMEM((N, 128), bf16),
            pltpu.VMEM((N, 128), bf16),
            pltpu.VMEM(planes, bf16),
            pltpu.VMEM(planes, bf16),
            pltpu.VMEM(planes, bf16),
            pltpu.VMEM((N, 128), bf16),
            pltpu.VMEM(planes, bf16),
            pltpu.VMEM((N, 128), bf16),
            pltpu.VMEM(pairs, bf16),
            pltpu.VMEM((Q, 512), bf16),
            pltpu.VMEM((Q, 512), bf16),
            pltpu.VMEM((2 * Q, 512), f32),
            pltpu.VMEM((2, 3 * Q, 128), f32),
            pltpu.VMEM((2, 3 * Q, 128), f32),
            pltpu.VMEM((2, ROWS, N), f32),
            pltpu.VMEM((2, ROWS, N), f32),
            pltpu.SMEM((DEPTH,), jnp.int32),
            pltpu.SemaphoreType.DMA((6,)),
            pltpu.SemaphoreType.DMA((6,)),
            pltpu.SemaphoreType.DMA((6,)),
            pltpu.SemaphoreType.REGULAR,
        ],
        compiler_params=pltpu.CompilerParams(collective_id=0, has_side_effects=True, vmem_limit_bytes=48 << 20),
        name="continuation",
    )(
        *(
            pltpu.with_memory_space_constraint(value, pltpu.HBM)
            for value in (
                jnp.asarray(stacked),
                jnp.asarray(flipped),
                flight_fields.reshape(pairs),
                top_fields.reshape(pairs),
                slowness.reshape(ROWS, N),
                flight_blocks,
            )
        ),
        ref_slowness,
        top_block,
    )
    out = pl.BlockSpec(memory_space=pltpu.HBM)
    image, after_second = pl.pallas_call(
        store,
        out_shape=(jax.ShapeDtypeStruct((ROWS, N), f32), jax.ShapeDtypeStruct(pairs, bf16)),
        in_specs=[vmem, vmem],
        out_specs=(out, out),
        scratch_shapes=[pltpu.SemaphoreType.DMA((2,))],
        compiler_params=pltpu.CompilerParams(vmem_limit_bytes=2 << 20),
        name="store",
    )(image, after_second)
    return image[None], after_second.reshape(1, 2, 2, ROWS, N)


def solution(mesh):
    placed = (
        P("depth", None, None, "trans", None),
        P(None, None, "trans", None),
        P("depth", "trans", None),
        P("depth"),
        P(),
        P(),
    )
    return jax.shard_map(
        per_device,
        mesh=mesh,
        in_specs=placed,
        out_specs=(P("depth", "trans", None), P("depth", None, None, "trans", None)),
        check_vma=False,
    )
```
